512 devices in a mesh: blk: 64 (over x, y, core), spec: 8 (over z).
Axes of the slice: x: 4, y: 8, z: 8, core: 2. Of those that a mesh axis runs over, the one named last changes fastest.
Arguments:
- spectrum: float32 [32, 24, 65536], P('spec', None, 'blk'), may hold values from 0.05 to 2
- depths: float32 [65536], P('blk'), may hold values from 5 to 4000
- currents: float32 [2, 65536], P(None, 'blk'), may hold values from -4 to 4
- slopes: float32 [2, 65536], P(None, 'blk'), may hold values from -0.12 to 0.12
- wind_speed: float32 [2, 65536], P(None, 'blk'), may hold values from -40 to 40
- wet_mask: int32 [65536], P('blk'), may hold values 0 or 1
- face_owner: int32 [4096, 1], P('blk'), may hold values from 0 to 63, as said below
- face_block: int32 [4096], P('blk'), may hold values from 0 to 15
- freq_weights: bfloat16 [2, 32, 32], replicated, may hold values from 0.0049743652 to 0.079589844
- angle_weights: bfloat16 [2, 2, 24, 24], replicated, may hold values from 0.0049743652 to 0.099609375
- transfer_rate: float32 [32], replicated, may hold values from 0.05 to 0.3
Outputs:
- next_spectrum: float32 [32, 24, 65536], P('spec', None, 'blk')
The draws below stay inside these ranges and needn't reach their ends.
Inputs may be any that keep to these rules, and one draw needn't show every extreme that they name: `face_owner`: face i of one device is side i % 4 (west, east, south, north) of its block i // 4. Of the 64 rows of one device, 32 name another index and the rest name the device itself; no other index is named more than 2 times in those rows, and one is named exactly 2 times.
All inputs are finite; a program needn't handle non-finite values. No bound on the sum of `wet_mask` on one device may be relied on, other than what follows from the above.
Results may differ from the reference program's by a relative error of at most 0.0011.
The reference program's roundings to bfloat16 on the way count: a program that leaves them out, or rounds other values in their place, can miss the bound.
Values may be sent and summed in bfloat16 or wider, within the bound.
A program may use at most 64 MiB of HBM per device.

```python
import math
import jax
import jax.numpy as jnp
from jax import lax

FREQ = 32
DIRS = 24
TILE = 8
BLK_DEV = 16
FACES_DEV = 64
PTS_DEV = 1024
FACES = 4096
POINTS = 65536
CAP = 2
N_BLK = 64


def draw_face_owner(key, part):
    remote_count = 2 * BLK_DEV

    def one_device(device):
        device_key = jax.random.fold_in(key, device)
        start = jax.random.randint(jax.random.fold_in(device_key, 11), (), 0, N_BLK - 1, dtype=jnp.int32)
        slot = jnp.arange(remote_count, dtype=jnp.int32)
        group = slot // CAP
        offset = 1 + (group + start) % (N_BLK - 1)
        remote = (device + offset) % N_BLK
        own_part = jnp.zeros((FACES_DEV - remote_count,), jnp.int32) + device
        owners = jnp.concatenate([remote, own_part])
        placing = jax.random.permutation(jax.random.fold_in(device_key, 23), FACES_DEV)
        return owners[placing]
    every = jax.vmap(one_device)(jnp.arange(N_BLK, dtype=jnp.int32))
    return every.reshape(FACES, 1).astype(jnp.int32)


def with_ends(values, rng, least, high):
    longest = values.shape.index(max(values.shape))
    spots = []
    for shift in (0, 1):
        where = [jax.random.randint(jax.random.fold_in(rng, axis), (), 0, length) for axis, length in enumerate(values.shape)]
        where[longest] = (where[longest] + shift) % values.shape[longest]
        spots.append(tuple(where))
    return values.at[spots[0]].set(least).at[spots[1]].set(high)


def level_of(key, dims, cuts, smallest, largest):
    loudness = 1.0
    for position, shards_of in cuts:
        heights = jax.random.uniform(jax.random.fold_in(jax.random.fold_in(key, 6), position), (shards_of,), jnp.float32, smallest / len(cuts), largest / len(cuts))
        loudness = loudness * jnp.repeat(jnp.exp(heights), dims[position] // shards_of).reshape((-1,) + (1,) * (len(dims) - 1 - position))
    return loudness


def normal_values(stream_key, extent, scale, bound, shards=(), held_as=jnp.bfloat16):
    level = level_of(stream_key, extent, shards, -0.22, 0.18) if shards else 1.0
    drawn = jax.random.normal(stream_key, extent, jnp.float32) * scale * level
    return jnp.minimum(jnp.maximum(drawn, -bound), bound).astype(held_as)


def setup_inputs(seed: int = 0) -> dict:
    streams_of = jax.random.split(jax.random.key(seed), 12)
    return {
        "spectrum": jnp.clip(jnp.exp(math.log(2.0) - 3.6888794 * jax.random.uniform(streams_of[0], (FREQ, DIRS, POINTS), jnp.float32) ** level_of(streams_of[0], (FREQ, DIRS, POINTS), ((0, 8), (2, 64)), -0.2, 0.2)), 0.05, 2.0),
        "depths": jnp.clip(jnp.exp(math.log(4000.0) - 6.684612 * jax.random.uniform(streams_of[1], (POINTS,), jnp.float32) ** level_of(streams_of[1], (POINTS,), ((0, 64),), -0.2, 0.2)), 5.0, 4000.0),
        "currents": normal_values(streams_of[2], (2, POINTS), 1.0, 4.0, ((1, 64),), jnp.float32),
        "slopes": normal_values(streams_of[3], (2, POINTS), 0.02, 0.12, ((1, 64),), jnp.float32),
        "wind_speed": normal_values(streams_of[4], (2, POINTS), 8.0, 40.0, ((1, 64),), jnp.float32),
        "wet_mask": with_ends((jax.random.randint(streams_of[5], (POINTS,), 0, 8) < 7).astype(jnp.int32), jax.random.fold_in(streams_of[5], 1), 0, 1),
        "face_owner": draw_face_owner(jax.random.fold_in(streams_of[11], 71), 0),
        "face_block": with_ends(jax.random.randint(streams_of[7], (FACES,), 0, BLK_DEV), jax.random.fold_in(streams_of[7], 1), 0, BLK_DEV - 1).astype(jnp.int32),
        "freq_weights": jnp.clip(jnp.exp(jax.random.uniform(streams_of[8], (2, FREQ, FREQ), jnp.float32, math.log(0.0049743652), math.log(0.079589844))), 0.0049743652, 0.079589844).astype(jnp.bfloat16),
        "angle_weights": jnp.clip(jnp.exp(jax.random.uniform(streams_of[9], (2, 2, DIRS, DIRS), jnp.float32, math.log(0.0049743652), math.log(0.099609375))), 0.0049743652, 0.099609375).astype(jnp.bfloat16),
        "transfer_rate": jnp.clip(jnp.exp(jax.random.uniform(streams_of[10], (FREQ,), jnp.float32, math.log(0.05), math.log(0.3))), 0.05, 0.3),
    }


GRAVITY = 9.81
TIME_STEP = 200.0
CELL_SIZE = 5500.0
LOWEST_FREQ = 0.0418
FREQ_GROWTH = 1.1
WIND_GROWTH = 0.0003
TURN_LIMIT = 0.9

def dispersion(radian_freq, water_depth):
    deep_kh = radian_freq * radian_freq / GRAVITY * water_depth
    wave_kh = deep_kh / jnp.sqrt(jnp.tanh(deep_kh))
    decay_two = jnp.exp(-2.0 * wave_kh)
    denom_term = 1.0 - decay_two * decay_two
    shoal_ratio = 4.0 * wave_kh * decay_two / denom_term
    phase_speed = radian_freq * water_depth / wave_kh
    group_speed = 0.5 * (1.0 + shoal_ratio) * phase_speed
    turn_factor = 2.0 * radian_freq * decay_two / denom_term
    return (phase_speed, group_speed, turn_factor)

def courants(radian_freq, angle_values, water_depth, current_xy, slope_xy, wet_float):
    freq_column = radian_freq[:, None, None, None, None]
    phase_speed, group_speed, turn_factor = dispersion(freq_column, water_depth[None, None])
    cosine = jnp.cos(angle_values)[None, :, None, None, None]
    sine = jnp.sin(angle_values)[None, :, None, None, None]
    grid_ratio = TIME_STEP / CELL_SIZE
    cour_x = (group_speed * cosine + current_xy[0][None, None]) * grid_ratio * wet_float[None, None]
    cour_y = (group_speed * sine + current_xy[1][None, None]) * grid_ratio * wet_float[None, None]
    angle_step = 2.0 * math.pi / angle_values.shape[0]
    turning = turn_factor * (sine * slope_xy[0][None, None] - cosine * slope_xy[1][None, None]) * (TIME_STEP / angle_step)
    cour_turn = jnp.clip(turning, -TURN_LIMIT, TURN_LIMIT)
    return (phase_speed, cour_x, cour_y, cour_turn)

def edge_fluxes(wave_field, cour_x, cour_y):
    west_side = jnp.maximum(-cour_x[..., :, 0], 0.0) * wave_field[..., :, 0]
    east_side = jnp.maximum(cour_x[..., :, -1], 0.0) * wave_field[..., :, -1]
    south_side = jnp.maximum(-cour_y[..., 0, :], 0.0) * wave_field[..., 0, :]
    north_side = jnp.maximum(cour_y[..., -1, :], 0.0) * wave_field[..., -1, :]
    return jnp.stack([west_side, east_side, south_side, north_side], axis=3)

def transported(wave_field, cour_x, cour_y, cour_turn, inflow):
    tile_side = wave_field.shape[-1]
    rightward = jnp.maximum(cour_x, 0.0) * wave_field
    leftward = jnp.maximum(-cour_x, 0.0) * wave_field
    upward = jnp.maximum(cour_y, 0.0) * wave_field
    downward = jnp.maximum(-cour_y, 0.0) * wave_field
    lead_pads = [(0, 0)] * 3
    from_x = jnp.pad(rightward[..., :, :-1], lead_pads + [(0, 0), (1, 0)]) + jnp.pad(leftward[..., :, 1:], lead_pads + [(0, 0), (0, 1)])
    from_y = jnp.pad(upward[..., :-1, :], lead_pads + [(1, 0), (0, 0)]) + jnp.pad(downward[..., 1:, :], lead_pads + [(0, 1), (0, 0)])
    from_turn = jnp.roll(jnp.maximum(cour_turn, 0.0) * wave_field, 1, axis=1) + jnp.roll(jnp.maximum(-cour_turn, 0.0) * wave_field, -1, axis=1)
    ghost_x = jnp.pad(inflow[:, :, :, 0, :, None], lead_pads + [(0, 0), (0, tile_side - 1)])
    ghost_x = ghost_x + jnp.pad(inflow[:, :, :, 1, :, None], lead_pads + [(0, 0), (tile_side - 1, 0)])
    ghost_y = jnp.pad(inflow[:, :, :, 2, None, :], lead_pads + [(0, tile_side - 1), (0, 0)])
    ghost_y = ghost_y + jnp.pad(inflow[:, :, :, 3, None, :], lead_pads + [(tile_side - 1, 0), (0, 0)])
    outflow = (jnp.abs(cour_x) + jnp.abs(cour_y) + jnp.abs(cour_turn)) * wave_field
    return wave_field - outflow + from_x + from_y + from_turn + ghost_x + ghost_y

def rounded(values):
    return lax.optimization_barrier(values.astype(jnp.bfloat16)).astype(jnp.float32)

def nonlinear(levels, freq_weights, angle_weights, transfer_rate):
    levels_wide = levels.astype(jnp.float32)
    freq_wide = freq_weights.astype(jnp.float32)
    angle_wide = angle_weights.astype(jnp.float32)
    shifted_plus = rounded(jnp.einsum('gf,fdq->gdq', freq_wide[0], levels_wide))
    shifted_minus = rounded(jnp.einsum('gf,fdq->gdq', freq_wide[1], levels_wide))
    rate_column = transfer_rate[:, None, None]
    delta_list = []
    for mirror in range(2):
        image_plus = jnp.einsum('ed,gdq->geq', angle_wide[mirror, 0], shifted_plus)
        image_minus = jnp.einsum('ed,gdq->geq', angle_wide[mirror, 1], shifted_minus)
        delta_list.append(rate_column * (levels_wide * levels_wide * (image_plus + image_minus) - 2.0 * levels_wide * image_plus * image_minus))
    low_first = rounded(delta_list[0])
    low_second = rounded(delta_list[1])
    back_plus = rounded(jnp.einsum('ed,geq->gdq', angle_wide[0, 0], low_first) + jnp.einsum('ed,geq->gdq', angle_wide[1, 0], low_second))
    back_minus = rounded(jnp.einsum('ed,geq->gdq', angle_wide[0, 1], low_first) + jnp.einsum('ed,geq->gdq', angle_wide[1, 1], low_second))
    return -2.0 * (delta_list[0] + delta_list[1]) + jnp.einsum('gf,gdq->fdq', freq_wide[0], back_plus) + jnp.einsum('gf,gdq->fdq', freq_wide[1], back_minus)

def reference(spectrum, depths, currents, slopes, wind_speed, wet_mask, face_owner, face_block, freq_weights, angle_weights, transfer_rate):
    block_total = POINTS // (TILE * TILE)
    shape_five = (FREQ, DIRS, block_total, TILE, TILE)
    wave_field = spectrum.reshape(shape_five)
    freq_index = jnp.arange(FREQ, dtype=jnp.int32).astype(jnp.float32)
    radian_freq = 2.0 * math.pi * LOWEST_FREQ * jnp.power(jnp.float32(FREQ_GROWTH), freq_index)
    angle_values = jnp.arange(DIRS, dtype=jnp.int32).astype(jnp.float32) * (2.0 * math.pi / DIRS)
    wet_float = wet_mask.astype(jnp.float32)
    phase_speed, cour_x, cour_y, cour_turn = courants(radian_freq, angle_values, depths.reshape(block_total, TILE, TILE), currents.reshape(2, block_total, TILE, TILE), slopes.reshape(2, block_total, TILE, TILE), wet_float.reshape(block_total, TILE, TILE))
    edges = edge_fluxes(wave_field, cour_x, cour_y).reshape(FREQ, DIRS, block_total * 4, TILE)
    face_sides = jnp.arange(FACES, dtype=jnp.int32) % 4
    neighbour = (face_owner[:, 0] * BLK_DEV + face_block) * 4 + jnp.bitwise_xor(face_sides, 1)
    inflow = jnp.take(edges, neighbour, axis=2).reshape(FREQ, DIRS, block_total, 4, TILE)
    moved = transported(wave_field, cour_x, cour_y, cour_turn, inflow).reshape(FREQ, DIRS, POINTS)
    levels = moved.astype(jnp.bfloat16)
    pieces = levels.reshape(FREQ, DIRS, N_BLK, PTS_DEV).transpose(2, 0, 1, 3)
    transfer = lax.map(lambda block_piece: nonlinear(block_piece, freq_weights, angle_weights, transfer_rate), pieces)
    transfer = transfer.transpose(1, 2, 0, 3).reshape(FREQ, DIRS, POINTS)
    along_wind = wind_speed[0][None, None, :] * jnp.cos(angle_values)[None, :, None] + wind_speed[1][None, None, :] * jnp.sin(angle_values)[None, :, None]
    phase_flat = phase_speed.reshape(FREQ, 1, POINTS)
    growth = TIME_STEP * WIND_GROWTH * radian_freq[:, None, None] * jnp.maximum(along_wind / phase_flat - 1.0, 0.0)
    return wet_float[None, None, :] * (moved + transfer + growth * moved)
```

```python
import math

import jax
import jax.numpy as jnp
from jax import lax
from jax.experimental import pallas as pl
from jax.experimental.pallas import tpu as pltpu
from jax.sharding import PartitionSpec as P

MESH = pl.DeviceIdType.MESH
F32, BF16, I32 = jnp.float32, jnp.bfloat16, jnp.int32

GRAVITY = 9.81
TIME_STEP = 200.0
CELL_SIZE = 5500.0
LOWEST_FREQ = 0.0418
FREQ_GROWTH = 1.1
WIND_GROWTH = 0.0003
TURN_LIMIT = 0.9

FREQS, FL, DIRS, PTS, LANES = 32, 4, 24, 1024, 128
ROWS = FL * DIRS
NB, NZ, NBLK, NFACE = 64, 8, 16, 64
NCH = PTS // LANES
GRP = 8 * DIRS
EDGE_SCALE = 26000.0
CODE_MAX = 32767.0
PEAK_SCALE = 1024.0


def iota(shape, axis):
    return lax.broadcasted_iota(I32, shape, axis)


def dot(a, b):
    return jnp.dot(a, b, preferred_element_type=F32)


def dot_nt(a, b):
    return lax.dot_general(a, b, (((1,), (1,)), ((), ())), preferred_element_type=F32)


def by_direction(x):
    return [x.reshape(FREQS, 3, 8, LANES)[:, t].reshape(FREQS * 8, LANES) for t in range(3)]


def to_freq_form(x):
    return jnp.concatenate(by_direction(x), axis=1)


def from_freq_form(x):
    parts = [x[:, t * LANES:(t + 1) * LANES].reshape(FREQS, 1, 8, LANES) for t in range(3)]
    return jnp.concatenate(parts, axis=1).reshape(FREQS * DIRS, LANES)


def to_angle_form(x):
    return jnp.concatenate([x[g * GRP:(g + 1) * GRP] for g in range(4)], axis=1)


def from_angle_form(x):
    return jnp.concatenate([x[:, g * LANES:(g + 1) * LANES] for g in range(4)], axis=0)


def kernel(
    field_hbm, depth_ref, cur_ref, slope_ref, wind_ref, wet_ref, owner_ref, block_ref, fw_ref, aw_ref, rate_ref,
    out_ref,
    field, mv, g1, wetr, lev, lrecv, pool, trw, trs, reqs, reqr, req_sm, ridx, ridx_sm, esend, erecv,
    tsend, trecv, ssend, srecv, kf, kt, bd, bt, ratew, shoal,
    in_sem, sm_sem, q_send, q_recv, e_send, e_recv, l_send, l_recv, t_send, t_recv, s_send, s_recv,
):
    me = lax.axis_index("blk")
    z = lax.axis_index("spec")
    barrier = pltpu.get_barrier_semaphore()

    load = pltpu.make_async_copy(field_hbm, field, in_sem)
    load.start()

    def greet_blk(j, c):
        pl.semaphore_signal(barrier, inc=1, device_id={"blk": lax.rem(me + j, NB)}, device_id_type=MESH)
        return c

    def greet_spec(j, c):
        pl.semaphore_signal(barrier, inc=1, device_id={"spec": lax.rem(z + j, NZ)}, device_id_type=MESH)
        return c

    lax.fori_loop(1, NB, greet_blk, 0)
    lax.fori_loop(1, NZ, greet_spec, 0)

    own = owner_ref[...]
    ri, ci = iota((NFACE, NFACE), 0), iota((NFACE, NFACE), 1)
    ol = jnp.broadcast_to(own, (NFACE, NFACE))
    os = jnp.sum(jnp.where(ri == ci, ol, 0), axis=1, keepdims=True)
    same = jnp.where(os == ol, 1, 0)
    rank = jnp.sum(jnp.where(ri < ci, same, 0), axis=0, keepdims=True)
    lane = iota((1, NFACE), 1)
    wanted = (block_ref[...] * 4 + jnp.bitwise_xor(jnp.bitwise_and(lane, 3), 1))
    hit = jnp.where(ol == ri, 1, 0)
    first = jnp.where(rank == 0, wanted, 0)
    second = jnp.where(rank == 1, wanted, 0)
    ask0 = jnp.sum(hit * first, axis=1, keepdims=True)
    ask1 = jnp.sum(hit * second, axis=1, keepdims=True)
    li = iota((NFACE, LANES), 1)
    asks = jnp.where(li == 0, ask0, jnp.where(li == 1, ask1, 0))
    for p in range(NB):
        reqs[p] = asks[p:p + 1, :]
    zpad = jnp.zeros((1, LANES - NFACE), I32)
    si = iota((8, LANES), 0)
    wide = [jnp.concatenate([v, zpad], axis=1) for v in (own, jnp.bitwise_and(rank, 1) * 16, wanted)]
    table = jnp.where(si == 0, wide[0], jnp.where(si == 1, wide[1], jnp.where(si == 2, wide[2], 0)))
    ridx[...] = table
    move_idx = pltpu.make_async_copy(ridx, ridx_sm, sm_sem.at[0])
    move_idx.start()

    pl.semaphore_wait(barrier, NB - 1 + NZ - 1)

    def ask(j, c):
        p = lax.rem(me + j, NB)
        pltpu.make_async_remote_copy(
            src_ref=reqs.at[p], dst_ref=reqr.at[me], send_sem=q_send, recv_sem=q_recv,
            device_id={"blk": p}, device_id_type=MESH,
        ).start()
        return c

    lax.fori_loop(1, NB, ask, 0)

    depth = depth_ref[...]
    base_index = (z * FL).astype(F32)
    freqs = []
    for f in range(FL):
        power = jnp.exp((jnp.full((8, LANES), f, F32) + base_index) * math.log(FREQ_GROWTH))
        rf = power * (2.0 * math.pi * LOWEST_FREQ)
        deep = rf * rf / GRAVITY * depth
        kh = deep / jnp.sqrt(jnp.tanh(deep))
        decay = jnp.exp(-2.0 * kh)
        denom = 1.0 - decay * decay
        phase = rf * depth / kh
        shoal[0, f] = 0.5 * (1.0 + 4.0 * kh * decay / denom) * phase
        shoal[1, f] = 2.0 * rf * decay / denom
        shoal[2, f] = 1.0 / phase
        freqs.append(rf[0:1, :])
    angle = iota((DIRS, LANES), 0).astype(F32) * (2.0 * math.pi / DIRS)
    cosine, sine = jnp.cos(angle), jnp.sin(angle)
    grid_ratio = TIME_STEP / CELL_SIZE
    turn_ratio = TIME_STEP / (2.0 * math.pi / DIRS)
    shape = (FL, DIRS, LANES)
    lane3 = iota(shape, 2)
    col = jnp.bitwise_and(lane3, 7)
    row = jnp.bitwise_and(lax.shift_right_logical(lane3, 3), 7)
    rfcol = jnp.concatenate([f.reshape(1, 1, LANES) for f in freqs], axis=0)
    load.wait()
    pad_rows = jnp.zeros((LANES - ROWS, LANES), F32)
    for k in range(NCH):
        sl = slice(k * LANES, (k + 1) * LANES)
        e = field[:, :, sl]
        wet = wet_ref[k:k + 1, :].astype(F32)
        group = shoal[0, :, k:k + 1, :]
        turnf = shoal[1, :, k:k + 1, :]
        slow = shoal[2, :, k:k + 1, :]
        cx = (group * cosine[None] + cur_ref[0:1, sl][None]) * grid_ratio * wet[None]
        cy = (group * sine[None] + cur_ref[1:2, sl][None]) * grid_ratio * wet[None]
        bend = sine * slope_ref[0:1, sl] - cosine * slope_ref[1:2, sl]
        ct = jnp.clip(turnf * bend[None] * turn_ratio, -TURN_LIMIT, TURN_LIMIT)
        right = jnp.maximum(cx, 0.0) * e
        left = jnp.maximum(-cx, 0.0) * e
        up = jnp.maximum(cy, 0.0) * e
        down = jnp.maximum(-cy, 0.0) * e
        ahead = jnp.maximum(ct, 0.0) * e
        back = jnp.maximum(-ct, 0.0) * e
        we = jnp.where(col == 0, left, jnp.where(col == 7, right, 0.0)).reshape(ROWS, LANES)
        sn = jnp.where(row == 0, down, jnp.where(row == 7, up, 0.0)).reshape(ROWS, LANES)
        trw[k, :LANES] = jnp.transpose(jnp.concatenate([we, pad_rows], axis=0))
        trs[k, :LANES] = jnp.transpose(jnp.concatenate([sn, pad_rows], axis=0))
        acc = e - (right + left + up + down + ahead + back)
        acc = acc + jnp.where(col == 0, 0.0, pltpu.roll(right, 1, axis=2))
        acc = acc + jnp.where(col == 7, 0.0, pltpu.roll(left, LANES - 1, axis=2))
        acc = acc + jnp.where(row == 0, 0.0, pltpu.roll(up, 8, axis=2))
        acc = acc + jnp.where(row == 7, 0.0, pltpu.roll(down, LANES - 8, axis=2))
        acc = acc + jnp.concatenate([ahead[:, DIRS - 1:], ahead[:, :DIRS - 1]], axis=1)
        acc = acc + jnp.concatenate([back[:, 1:], back[:, :1]], axis=1)
        mv[k] = acc.reshape(ROWS, LANES)
        along = wind_ref[0:1, sl] * cosine + wind_ref[1:2, sl] * sine
        grow = TIME_STEP * WIND_GROWTH * rfcol * jnp.maximum(along[None] * slow - 1.0, 0.0)
        g1[k] = (wet[None] * (1.0 + grow)).reshape(ROWS, LANES)
        wetr[k] = wet
        for b in range(2):
            base = b * 64
            idx = (2 * k + b) * 4
            pool[idx + 0] = trw[k, pl.ds(base, 8, stride=8), :]
            pool[idx + 1] = trw[k, pl.ds(base + 7, 8, stride=8), :]
            pool[idx + 2] = trs[k, base:base + 8, :]
            pool[idx + 3] = trs[k, base + 56:base + 64, :]

    pltpu.make_async_remote_copy(
        src_ref=reqs.at[pl.ds(0, NB - 1)], dst_ref=reqr.at[pl.ds(0, NB - 1)], send_sem=q_send, recv_sem=q_recv,
        device_id={"blk": me}, device_id_type=MESH,
    ).wait()
    reqr[me] = jnp.zeros((1, LANES), I32)
    move_req = pltpu.make_async_copy(reqr, req_sm, sm_sem.at[1])
    move_req.start()
    move_req.wait()

    def code(x):
        return jnp.minimum(x * EDGE_SCALE + 0.5, 65535.0).astype(I32)

    def pack(j, c):
        p = lax.rem(me + j, NB)
        a = code(pool[req_sm[p, 0, 0]])
        b = code(pool[req_sm[p, 0, 1]])
        esend[p] = jnp.bitwise_or(a, jnp.left_shift(b, 16))
        return c

    def give(j, c):
        p = lax.rem(me + j, NB)
        pltpu.make_async_remote_copy(
            src_ref=esend.at[p], dst_ref=erecv.at[me], send_sem=e_send, recv_sem=e_recv,
            device_id={"blk": p}, device_id_type=MESH,
        ).start()
        return c

    lax.fori_loop(1, NB, pack, 0)
    lax.fori_loop(1, NB, give, 0)

    spread = jnp.where(lax.shift_right_logical(iota((256, FREQS), 0), 3) == iota((256, FREQS), 1), 1.0, 0.0).astype(BF16)
    same_i = jnp.bitwise_and(iota((256, 256), 0), 7) == jnp.bitwise_and(iota((256, 256), 1), 7)
    for s in range(2):
        w = fw_ref[s]
        kf[s] = jnp.where(same_i, dot_nt(dot(spread, w).astype(BF16), spread), 0.0).astype(BF16)
        kt[s] = jnp.where(same_i, dot_nt(dot_nt(spread, w).astype(BF16), spread), 0.0).astype(BF16)

    def over(x):
        return lax.shift_right_logical(x * 2731, 16)

    r24 = iota((GRP, DIRS), 0)
    fan = jnp.where(r24 - DIRS * over(r24) == iota((GRP, DIRS), 1), 1.0, 0.0).astype(BF16)
    same_g = over(iota((GRP, GRP), 0)) == over(iota((GRP, GRP), 1))
    for m in range(2):
        for s in range(2):
            a = aw_ref[m, s]
            bd[m, s] = jnp.where(same_g, dot_nt(dot(fan, a).astype(BF16), fan), 0.0).astype(BF16)
            bt[m, s] = jnp.where(same_g, dot_nt(dot_nt(fan, a).astype(BF16), fan), 0.0).astype(BF16)
    for g in range(4):
        pick = over(iota((GRP, FREQS), 0)) + 8 * g == iota((GRP, FREQS), 1)
        column = jnp.sum(jnp.where(pick, rate_ref[...], 0.0), axis=1, keepdims=True)
        ratew[:, g * LANES:(g + 1) * LANES] = jnp.broadcast_to(column, (GRP, LANES))
    for k in range(NCH):
        trw[k, :LANES] = jnp.zeros((LANES, LANES), F32)
        trs[k, :LANES] = jnp.zeros((LANES, LANES), F32)
    erecv[me] = jnp.zeros((8, LANES), I32)
    move_idx.wait()

    pltpu.make_async_remote_copy(
        src_ref=esend.at[pl.ds(0, NB - 1)], dst_ref=erecv.at[pl.ds(0, NB - 1)], send_sem=e_send, recv_sem=e_recv,
        device_id={"blk": me}, device_id_type=MESH,
    ).wait()

    def face(j):
        owner = ridx_sm[0, j]
        got = jnp.bitwise_and(jnp.right_shift(erecv[owner], ridx_sm[1, j]), 65535)
        return jnp.where(owner != me, got.astype(F32) * (1.0 / EDGE_SCALE), pool[ridx_sm[2, j]])

    def finish(k):
        for b in range(2):
            base, j = b * 64, (2 * k + b) * 4
            trw[k, pl.ds(base, 8, stride=8), :] = face(j)
            trw[k, pl.ds(base + 7, 8, stride=8), :] = face(j + 1)
            trs[k, base:base + 8, :] = face(j + 2)
            trs[k, base + 56:base + 64, :] = face(j + 3)
        moved = mv[k] + jnp.transpose(trw[k, :LANES] + trs[k, :LANES])[:ROWS]
        mv[k] = moved
        return moved.astype(BF16)

    def level_copy(k):
        return pltpu.make_async_remote_copy(
            src_ref=lev.at[k], dst_ref=lrecv.at[z], send_sem=l_send.at[k], recv_sem=l_recv.at[z],
            device_id={"spec": k}, device_id_type=MESH,
        )

    for o in (4, 3, 5, 2, 6, 1, 7):
        k = lax.rem(z + o, NZ)
        lev[k] = finish(k)
        level_copy(k).start()
    lrecv[z] = finish(z)
    for k in range(NCH):
        g1[k] = mv[k] * g1[k]

    for o in range(1, NZ):
        k = lax.rem(z + o, NZ)
        pltpu.make_async_remote_copy(
            src_ref=lev.at[k], dst_ref=lrecv.at[k], send_sem=l_send.at[k], recv_sem=l_recv.at[k],
            device_id={"spec": k}, device_id_type=MESH,
        ).wait()

    levels = lrecv[...].reshape(FREQS * DIRS, LANES).astype(F32)
    level_f = to_freq_form(levels).astype(BF16)
    shifted = [to_angle_form(from_freq_form(dot(kf[s], level_f))).astype(BF16) for s in range(2)]
    level_a = to_angle_form(levels)
    square = level_a * level_a
    total = None
    lows = []
    for m in range(2):
        plus, minus = dot(bd[m, 0], shifted[0]), dot(bd[m, 1], shifted[1])
        delta = ratew[...] * (square * (plus + minus) - 2.0 * level_a * plus * minus)
        lows.append(delta.astype(BF16))
        total = delta if total is None else total + delta
    result = None
    for s in range(2):
        backs = dot(bt[0, s], lows[0]) + dot(bt[1, s], lows[1])
        term = dot(kt[s], to_freq_form(from_angle_form(backs)).astype(BF16))
        result = term if result is None else result + term
    result = from_freq_form(result) - 2.0 * from_angle_form(total)
    mv[...] = result.reshape(NZ, ROWS, LANES)

    def ret_copy(k):
        return pltpu.make_async_remote_copy(
            src_ref=tsend.at[k], dst_ref=trecv.at[z], send_sem=t_send.at[k], recv_sem=t_recv.at[z],
            device_id={"spec": k}, device_id_type=MESH,
        )

    def peak_copy(k):
        return pltpu.make_async_remote_copy(
            src_ref=ssend.at[k], dst_ref=srecv.at[z], send_sem=s_send.at[k], recv_sem=s_recv.at[z],
            device_id={"spec": k}, device_id_type=MESH,
        )

    for o in (4, 3, 5, 2, 6, 1, 7):
        k = lax.rem(z + o, NZ)
        t = mv[k]
        peak = jnp.max(jnp.abs(t), axis=0, keepdims=True)
        unit = (peak * PEAK_SCALE).astype(I32) + 1
        y = t * (CODE_MAX * PEAK_SCALE / unit.astype(F32))
        q = (y + jnp.where(y >= 0.0, 0.5, -0.5)).astype(I32)
        tsend[k] = jnp.bitwise_or(jnp.left_shift(q[:ROWS // 2], 16), jnp.bitwise_and(q[ROWS // 2:], 65535))
        ssend[k] = unit
        ret_copy(k).start()
        peak_copy(k).start()

    def emit(k, t):
        at = pl.ds(pl.multiple_of(k * LANES, LANES), LANES)
        out_ref[:, :, at] = (g1[k] + wetr[k] * t).reshape(FL, DIRS, LANES)

    emit(z, mv[z])
    for o in (1, 7, 2, 6, 3, 5, 4):
        k = lax.rem(z + o, NZ)
        for buf, dst, snd, rcv in ((tsend, trecv, t_send, t_recv), (ssend, srecv, s_send, s_recv)):
            pltpu.make_async_remote_copy(
                src_ref=buf.at[k], dst_ref=dst.at[k], send_sem=snd.at[k], recv_sem=rcv.at[k],
                device_id={"spec": k}, device_id_type=MESH,
            ).wait()
        w = trecv[k]
        scale = srecv[k].astype(F32) * (1.0 / (CODE_MAX * PEAK_SCALE))
        high = jnp.right_shift(w, 16).astype(F32)
        low = jnp.right_shift(jnp.left_shift(w, 16), 16).astype(F32)
        emit(k, jnp.concatenate([high, low], axis=0) * scale)


def shards(
    spectrum, depths, currents, slopes, wind_speed, wet_mask, face_owner, face_block,
    freq_weights, angle_weights, transfer_rate,
):
    vmem = pl.BlockSpec(memory_space=pltpu.VMEM)
    dma = pltpu.SemaphoreType.DMA
    return pl.pallas_call(
        kernel,
        out_shape=jax.ShapeDtypeStruct((FL, DIRS, PTS), F32),
        in_specs=[pl.BlockSpec(memory_space=pl.ANY)] + [vmem] * 10,
        out_specs=vmem,
        scratch_shapes=[
            pltpu.VMEM((FL, DIRS, PTS), F32),
            pltpu.VMEM((NCH, ROWS, LANES), F32),
            pltpu.VMEM((NCH, ROWS, LANES), F32),
            pltpu.VMEM((NCH, 1, LANES), F32),
            pltpu.VMEM((NCH, ROWS, LANES), BF16),
            pltpu.VMEM((NCH, ROWS, LANES), BF16),
            pltpu.VMEM((NFACE, 8, LANES), F32),
            pltpu.VMEM((NCH, LANES + 8, LANES), F32),
            pltpu.VMEM((NCH, LANES + 8, LANES), F32),
            pltpu.VMEM((NB, 1, LANES), I32),
            pltpu.VMEM((NB, 1, LANES), I32),
            pltpu.SMEM((NB, 1, LANES), I32),
            pltpu.VMEM((8, LANES), I32),
            pltpu.SMEM((8, LANES), I32),
            pltpu.VMEM((NB, 8, LANES), I32),
            pltpu.VMEM((NB, 8, LANES), I32),
            pltpu.VMEM((NZ, ROWS // 2, LANES), I32),
            pltpu.VMEM((NZ, ROWS // 2, LANES), I32),
            pltpu.VMEM((NZ, 1, LANES), I32),
            pltpu.VMEM((NZ, 1, LANES), I32),
            pltpu.VMEM((2, 256, 256), BF16),
            pltpu.VMEM((2, 256, 256), BF16),
            pltpu.VMEM((2, 2, GRP, GRP), BF16),
            pltpu.VMEM((2, 2, GRP, GRP), BF16),
            pltpu.VMEM((GRP, 4 * LANES), F32),
            pltpu.VMEM((3, FL, 8, LANES), F32),
            dma, dma((2,)), dma, dma, dma, dma,
            dma((NZ,)), dma((NZ,)), dma((NZ,)), dma((NZ,)), dma((NZ,)), dma((NZ,)),
        ],
        compiler_params=pltpu.CompilerParams(collective_id=0, has_side_effects=True),
    )(
        spectrum, depths.reshape(8, LANES), currents, slopes, wind_speed, wet_mask.reshape(8, LANES),
        face_owner.reshape(1, NFACE), face_block.reshape(1, NFACE), freq_weights, angle_weights,
        transfer_rate.reshape(1, FREQS),
    )


def solution(mesh):
    in_specs = (
        P("spec", None, "blk"), P("blk"), P(None, "blk"), P(None, "blk"), P(None, "blk"), P("blk"),
        P("blk", None), P("blk"), P(), P(), P(),
    )
    return jax.shard_map(
        shards, mesh=mesh, in_specs=in_specs, out_specs=P("spec", None, "blk"), check_vma=False
    )
```

```python
import math

import jax
import jax.numpy as jnp
from jax import lax
from jax.experimental import pallas as pl
from jax.experimental.pallas import tpu as pltpu
from jax.sharding import PartitionSpec as P

MESH = pl.DeviceIdType.MESH
FAR = (4, 3, 5, 2, 6, 1, 7, 0)
F32, BF16, I32 = jnp.float32, jnp.bfloat16, jnp.int32

GRAVITY = 9.81
TIME_STEP = 200.0
CELL_SIZE = 5500.0
LOWEST_FREQ = 0.0418
FREQ_GROWTH = 1.1
WIND_GROWTH = 0.0003
TURN_LIMIT = 0.9

FREQS, FL, DIRS, PTS, LANES = 32, 4, 24, 1024, 128
ROWS = FL * DIRS
NB, NZ, NBLK, NFACE = 64, 8, 16, 64
LAG = 4
NCH = PTS // LANES
GRP = 8 * DIRS
EDGE_SCALE = 26000.0
CODE_MAX = 32767.0
PEAK_SCALE = 1024.0


def iota(shape, axis):
    return lax.broadcasted_iota(I32, shape, axis)


def dot(a, b):
    return jnp.dot(a, b, preferred_element_type=F32)


def dot_nt(a, b):
    return lax.dot_general(a, b, (((1,), (1,)), ((), ())), preferred_element_type=F32)


def by_direction(x):
    return [x.reshape(FREQS, 3, 8, LANES)[:, t].reshape(FREQS * 8, LANES) for t in range(3)]


def to_freq_form(x):
    return jnp.concatenate(by_direction(x), axis=1)


def from_freq_form(x):
    parts = [x[:, t * LANES:(t + 1) * LANES].reshape(FREQS, 1, 8, LANES) for t in range(3)]
    return jnp.concatenate(parts, axis=1).reshape(FREQS * DIRS, LANES)


def to_angle_form(x):
    return jnp.concatenate([x[g * GRP:(g + 1) * GRP] for g in range(4)], axis=1)


def from_angle_form(x):
    return jnp.concatenate([x[:, g * LANES:(g + 1) * LANES] for g in range(4)], axis=0)


def kernel(
    field_hbm, depth_ref, cur_ref, slope_ref, wind_ref, wet_ref, owner_ref, block_ref, fw_ref, aw_ref, rate_ref,
    out_ref,
    field, mv, g1, wetr, lev, lrecv, pool, trw, trs, reqs, line_in, mid, plane_in, table, table_sm, ridx, ridx_sm, esend, erecv,
    tsend, trecv, ssend, srecv, kf, kt, bd, bt, ratew, shoal,
    in_sem, sm_sem, q_send, q_recv, r_send, r_recv, e_send, e_recv, l_send, l_recv, t_send, t_recv, s_send, s_recv,
):
    me = lax.axis_index("blk")
    z = lax.axis_index("spec")
    barrier = pltpu.get_barrier_semaphore()

    load = pltpu.make_async_copy(field_hbm, field, in_sem)
    load.start()

    x, y, c = me // 16, lax.rem(me // 2, 8), lax.rem(me, 2)
    q = x * 2 + c
    xs = [lax.rem(x + d, 4) * 16 for d in range(4)]
    ys = [lax.rem(y + d, 8) * 2 for d in range(8)]
    cs = [lax.rem(c + d, 2) for d in range(2)]
    plane = [(dx, dc) for dx in (2, 1, 3, 0) for dc in (1, 0) if dx or dc]

    for d in FAR[:-1]:
        for at in ({"blk": xs[0] + ys[d] + cs[0]}, {"spec": lax.rem(z + d, NZ)}):
            pl.semaphore_signal(barrier, inc=1, device_id=at, device_id_type=MESH)
    for dx, dc in plane:
        pl.semaphore_signal(barrier, inc=1, device_id={"blk": xs[dx] + ys[0] + cs[dc]}, device_id_type=MESH)

    own = owner_ref[...]
    ri, ci = iota((NFACE, NFACE), 0), iota((NFACE, NFACE), 1)
    ol = jnp.broadcast_to(own, (NFACE, NFACE))
    os = jnp.sum(jnp.where(ri == ci, ol, 0), axis=1, keepdims=True)
    same = jnp.where(os == ol, 1, 0)
    rank = jnp.sum(jnp.where(ri < ci, same, 0), axis=0, keepdims=True)
    lane = iota((1, NFACE), 1)
    wanted = (block_ref[...] * 4 + jnp.bitwise_xor(jnp.bitwise_and(lane, 3), 1))
    peer = jnp.bitwise_and(ri >> 1, 3) * 16 + (ri >> 3) * 2 + jnp.bitwise_and(ri, 1)
    hit = jnp.where(ol == peer, 1, 0)
    first = jnp.where(rank == 0, wanted, 0)
    second = jnp.where(rank == 1, wanted, 0)
    ask0 = jnp.sum(hit * first, axis=1, keepdims=True)
    ask1 = jnp.sum(hit * second, axis=1, keepdims=True)
    asks = jnp.where(iota((NFACE, LANES), 1) == me, ask0 + 64 * ask1, 0)
    for d in range(8):
        reqs[d] = asks[8 * d:8 * d + 8]
    zpad = jnp.zeros((1, LANES - NFACE), I32)
    si = iota((8, LANES), 0)
    wide = [jnp.concatenate([v, zpad], axis=1) for v in (own, jnp.bitwise_and(rank, 1) * 16, wanted)]
    faces = jnp.where(si == 0, wide[0], jnp.where(si == 1, wide[1], jnp.where(si == 2, wide[2], 0)))
    ridx[...] = faces
    move_idx = pltpu.make_async_copy(ridx, ridx_sm, sm_sem.at[0])
    move_idx.start()

    pl.semaphore_wait(barrier, 21)

    for d in FAR[:-1]:
        pltpu.make_async_remote_copy(
            src_ref=reqs.at[lax.rem(y + d, 8)], dst_ref=line_in.at[y], send_sem=q_send, recv_sem=q_recv,
            device_id={"blk": xs[0] + ys[d] + cs[0]}, device_id_type=MESH,
        ).start()
    line_in[y] = reqs[y]

    depth = depth_ref[...]
    base_index = (z * FL).astype(F32)
    freqs = []
    for f in range(FL):
        power = jnp.exp((jnp.full((8, LANES), f, F32) + base_index) * math.log(FREQ_GROWTH))
        rf = power * (2.0 * math.pi * LOWEST_FREQ)
        deep = rf * rf / GRAVITY * depth
        kh = deep / jnp.sqrt(jnp.tanh(deep))
        decay = jnp.exp(-2.0 * kh)
        denom = 1.0 - decay * decay
        phase = rf * depth / kh
        shoal[0, f] = 0.5 * (1.0 + 4.0 * kh * decay / denom) * phase
        shoal[1, f] = 2.0 * rf * decay / denom
        shoal[2, f] = 1.0 / phase
        freqs.append(rf[0:1, :])
    angle = iota((DIRS, LANES), 0).astype(F32) * (2.0 * math.pi / DIRS)
    cosine, sine = jnp.cos(angle), jnp.sin(angle)
    grid_ratio = TIME_STEP / CELL_SIZE
    turn_ratio = TIME_STEP / (2.0 * math.pi / DIRS)
    shape = (FL, DIRS, LANES)
    lane3 = iota(shape, 2)
    col = jnp.bitwise_and(lane3, 7)
    row = jnp.bitwise_and(lax.shift_right_logical(lane3, 3), 7)
    rfcol = jnp.concatenate([f.reshape(1, 1, LANES) for f in freqs], axis=0)
    load.wait()
    pad_rows = jnp.zeros((LANES - ROWS, LANES), F32)
    for k in range(NCH):
        sl = slice(k * LANES, (k + 1) * LANES)
        e = field[:, :, sl]
        wet = wet_ref[k:k + 1, :].astype(F32)
        group = shoal[0, :, k:k + 1, :]
        turnf = shoal[1, :, k:k + 1, :]
        slow = shoal[2, :, k:k + 1, :]
        cx = (group * cosine[None] + cur_ref[0:1, sl][None]) * grid_ratio * wet[None]
        cy = (group * sine[None] + cur_ref[1:2, sl][None]) * grid_ratio * wet[None]
        bend = sine * slope_ref[0:1, sl] - cosine * slope_ref[1:2, sl]
        ct = jnp.clip(turnf * bend[None] * turn_ratio, -TURN_LIMIT, TURN_LIMIT)
        right = jnp.maximum(cx, 0.0) * e
        left = jnp.maximum(-cx, 0.0) * e
        up = jnp.maximum(cy, 0.0) * e
        down = jnp.maximum(-cy, 0.0) * e
        ahead = jnp.maximum(ct, 0.0) * e
        back = jnp.maximum(-ct, 0.0) * e
        we = jnp.where(col == 0, left, jnp.where(col == 7, right, 0.0)).reshape(ROWS, LANES)
        sn = jnp.where(row == 0, down, jnp.where(row == 7, up, 0.0)).reshape(ROWS, LANES)
        trw[k, :LANES] = jnp.transpose(jnp.concatenate([we, pad_rows], axis=0))
        trs[k, :LANES] = jnp.transpose(jnp.concatenate([sn, pad_rows], axis=0))
        acc = e - (right + left + up + down + ahead + back)
        acc = acc + jnp.where(col == 0, 0.0, pltpu.roll(right, 1, axis=2))
        acc = acc + jnp.where(col == 7, 0.0, pltpu.roll(left, LANES - 1, axis=2))
        acc = acc + jnp.where(row == 0, 0.0, pltpu.roll(up, 8, axis=2))
        acc = acc + jnp.where(row == 7, 0.0, pltpu.roll(down, LANES - 8, axis=2))
        acc = acc + jnp.concatenate([ahead[:, DIRS - 1:], ahead[:, :DIRS - 1]], axis=1)
        acc = acc + jnp.concatenate([back[:, 1:], back[:, :1]], axis=1)
        mv[k] = acc.reshape(ROWS, LANES)
        along = wind_ref[0:1, sl] * cosine + wind_ref[1:2, sl] * sine
        grow = TIME_STEP * WIND_GROWTH * rfcol * jnp.maximum(along[None] * slow - 1.0, 0.0)
        g1[k] = (wet[None] * (1.0 + grow)).reshape(ROWS, LANES)
        wetr[k] = wet
        for b in range(2):
            base = b * 64
            idx = (2 * k + b) * 4
            pool[idx + 0] = trw[k, pl.ds(base, 8, stride=8), :]
            pool[idx + 1] = trw[k, pl.ds(base + 7, 8, stride=8), :]
            pool[idx + 2] = trs[k, base:base + 8, :]
            pool[idx + 3] = trs[k, base + 56:base + 64, :]

    pltpu.make_async_remote_copy(
        src_ref=reqs.at[pl.ds(0, 7)], dst_ref=line_in.at[pl.ds(0, 7)], send_sem=q_send, recv_sem=q_recv,
        device_id={"blk": me}, device_id_type=MESH,
    ).wait()
    gathered = jnp.sum(line_in[...], axis=0)
    for d in range(8):
        mid[d] = gathered[d:d + 1]
    for dx, dc in plane:
        pltpu.make_async_remote_copy(
            src_ref=mid.at[lax.rem(x + dx, 4) * 2 + cs[dc]], dst_ref=plane_in.at[q], send_sem=r_send, recv_sem=r_recv,
            device_id={"blk": xs[dx] + ys[0] + cs[dc]}, device_id_type=MESH,
        ).start()
    plane_in[q] = mid[q]
    pltpu.make_async_remote_copy(
        src_ref=mid.at[pl.ds(0, 7)], dst_ref=plane_in.at[pl.ds(0, 7)], send_sem=r_send, recv_sem=r_recv,
        device_id={"blk": me}, device_id_type=MESH,
    ).wait()
    table[...] = jnp.sum(plane_in[...], axis=0)
    move_req = pltpu.make_async_copy(table, table_sm, sm_sem.at[1])
    move_req.start()
    move_req.wait()

    def code(v):
        return jnp.minimum(v * EDGE_SCALE + 0.5, 65535.0).astype(I32)

    def give(step, p):
        pltpu.make_async_remote_copy(
            src_ref=esend.at[step], dst_ref=erecv.at[me], send_sem=e_send, recv_sem=e_recv,
            device_id={"blk": p}, device_id_type=MESH,
        ).start()

    order = [(dx, dy, dc) for dc in (1, 0) for dx in (2, 1, 3, 0) for dy in FAR if dx or dy or dc]
    ready = []
    for step, (dx, dy, dc) in enumerate(order):
        p = xs[dx] + ys[dy] + cs[dc]
        ids = table_sm[0, p]
        a = code(pool[jnp.bitwise_and(ids, 63)])
        b = code(pool[jnp.bitwise_and(jnp.right_shift(ids, 6), 63)])
        esend[step] = jnp.bitwise_or(a, jnp.left_shift(b, 16))
        ready.append((step, p))
        if len(ready) > LAG:
            give(*ready.pop(0))
    for item in ready:
        give(*item)

    spread = jnp.where(lax.shift_right_logical(iota((256, FREQS), 0), 3) == iota((256, FREQS), 1), 1.0, 0.0).astype(BF16)
    same_i = jnp.bitwise_and(iota((256, 256), 0), 7) == jnp.bitwise_and(iota((256, 256), 1), 7)
    for s in range(2):
        w = fw_ref[s]
        kf[s] = jnp.where(same_i, dot_nt(dot(spread, w).astype(BF16), spread), 0.0).astype(BF16)
        kt[s] = jnp.where(same_i, dot_nt(dot_nt(spread, w).astype(BF16), spread), 0.0).astype(BF16)

    def over(x):
        return lax.shift_right_logical(x * 2731, 16)

    r24 = iota((GRP, DIRS), 0)
    fan = jnp.where(r24 - DIRS * over(r24) == iota((GRP, DIRS), 1), 1.0, 0.0).astype(BF16)
    same_g = over(iota((GRP, GRP), 0)) == over(iota((GRP, GRP), 1))
    for m in range(2):
        for s in range(2):
            a = aw_ref[m, s]
            bd[m, s] = jnp.where(same_g, dot_nt(dot(fan, a).astype(BF16), fan), 0.0).astype(BF16)
            bt[m, s] = jnp.where(same_g, dot_nt(dot_nt(fan, a).astype(BF16), fan), 0.0).astype(BF16)
    for g in range(4):
        pick = over(iota((GRP, FREQS), 0)) + 8 * g == iota((GRP, FREQS), 1)
        column = jnp.sum(jnp.where(pick, rate_ref[...], 0.0), axis=1, keepdims=True)
        ratew[:, g * LANES:(g + 1) * LANES] = jnp.broadcast_to(column, (GRP, LANES))
    for k in range(NCH):
        trw[k, :LANES] = jnp.zeros((LANES, LANES), F32)
        trs[k, :LANES] = jnp.zeros((LANES, LANES), F32)
    erecv[me] = jnp.zeros((8, LANES), I32)
    move_idx.wait()

    pltpu.make_async_remote_copy(
        src_ref=esend.at[pl.ds(0, NB - 1)], dst_ref=erecv.at[pl.ds(0, NB - 1)], send_sem=e_send, recv_sem=e_recv,
        device_id={"blk": me}, device_id_type=MESH,
    ).wait()

    def face(j):
        owner = ridx_sm[0, j]
        got = jnp.bitwise_and(jnp.right_shift(erecv[owner], ridx_sm[1, j]), 65535)
        return jnp.where(owner != me, got.astype(F32) * (1.0 / EDGE_SCALE), pool[ridx_sm[2, j]])

    def finish(k):
        for b in range(2):
            base, j = b * 64, (2 * k + b) * 4
            trw[k, pl.ds(base, 8, stride=8), :] = face(j)
            trw[k, pl.ds(base + 7, 8, stride=8), :] = face(j + 1)
            trs[k, base:base + 8, :] = face(j + 2)
            trs[k, base + 56:base + 64, :] = face(j + 3)
        moved = mv[k] + jnp.transpose(trw[k, :LANES] + trs[k, :LANES])[:ROWS]
        mv[k] = moved
        return moved.astype(BF16)

    def level_copy(k):
        return pltpu.make_async_remote_copy(
            src_ref=lev.at[k], dst_ref=lrecv.at[z], send_sem=l_send.at[k], recv_sem=l_recv.at[z],
            device_id={"spec": k}, device_id_type=MESH,
        )

    previous = None
    for o in FAR[:-1]:
        k = lax.rem(z + o, NZ)
        lev[k] = finish(k)
        if previous is not None:
            level_copy(previous).start()
        previous = k
    level_copy(previous).start()
    lrecv[z] = finish(z)
    for k in range(NCH):
        g1[k] = mv[k] * g1[k]

    for o in range(1, NZ):
        k = lax.rem(z + o, NZ)
        pltpu.make_async_remote_copy(
            src_ref=lev.at[k], dst_ref=lrecv.at[k], send_sem=l_send.at[k], recv_sem=l_recv.at[k],
            device_id={"spec": k}, device_id_type=MESH,
        ).wait()

    levels = lrecv[...].reshape(FREQS * DIRS, LANES).astype(F32)
    level_f = to_freq_form(levels).astype(BF16)
    shifted = [to_angle_form(from_freq_form(dot(kf[s], level_f))).astype(BF16) for s in range(2)]
    level_a = to_angle_form(levels)
    square = level_a * level_a
    total = None
    lows = []
    for m in range(2):
        plus, minus = dot(bd[m, 0], shifted[0]), dot(bd[m, 1], shifted[1])
        delta = ratew[...] * (square * (plus + minus) - 2.0 * level_a * plus * minus)
        lows.append(delta.astype(BF16))
        total = delta if total is None else total + delta
    result = None
    for s in range(2):
        backs = dot(bt[0, s], lows[0]) + dot(bt[1, s], lows[1])
        term = dot(kt[s], to_freq_form(from_angle_form(backs)).astype(BF16))
        result = term if result is None else result + term
    result = from_freq_form(result) - 2.0 * from_angle_form(total)
    mv[...] = result.reshape(NZ, ROWS, LANES)

    def ret_copy(k):
        return pltpu.make_async_remote_copy(
            src_ref=tsend.at[k], dst_ref=trecv.at[z], send_sem=t_send.at[k], recv_sem=t_recv.at[z],
            device_id={"spec": k}, device_id_type=MESH,
        )

    def peak_copy(k):
        return pltpu.make_async_remote_copy(
            src_ref=ssend.at[k], dst_ref=srecv.at[z], send_sem=s_send.at[k], recv_sem=s_recv.at[z],
            device_id={"spec": k}, device_id_type=MESH,
        )

    for o in (4, 3, 5, 2, 6, 1, 7):
        k = lax.rem(z + o, NZ)
        t = mv[k]
        peak = jnp.max(jnp.abs(t), axis=0, keepdims=True)
        unit = (peak * PEAK_SCALE).astype(I32) + 1
        y = t * (CODE_MAX * PEAK_SCALE / unit.astype(F32))
        q = (y + jnp.where(y >= 0.0, 0.5, -0.5)).astype(I32)
        tsend[k] = jnp.bitwise_or(jnp.left_shift(q[:ROWS // 2], 16), jnp.bitwise_and(q[ROWS // 2:], 65535))
        ssend[k] = unit
        ret_copy(k).start()
        peak_copy(k).start()

    def emit(k, t):
        at = pl.ds(pl.multiple_of(k * LANES, LANES), LANES)
        out_ref[:, :, at] = (g1[k] + wetr[k] * t).reshape(FL, DIRS, LANES)

    emit(z, mv[z])
    for o in (1, 7, 2, 6, 3, 5, 4):
        k = lax.rem(z + o, NZ)
        for buf, dst, snd, rcv in ((tsend, trecv, t_send, t_recv), (ssend, srecv, s_send, s_recv)):
            pltpu.make_async_remote_copy(
                src_ref=buf.at[k], dst_ref=dst.at[k], send_sem=snd.at[k], recv_sem=rcv.at[k],
                device_id={"spec": k}, device_id_type=MESH,
            ).wait()
        w = trecv[k]
        scale = srecv[k].astype(F32) * (1.0 / (CODE_MAX * PEAK_SCALE))
        high = jnp.right_shift(w, 16).astype(F32)
        low = jnp.right_shift(jnp.left_shift(w, 16), 16).astype(F32)
        emit(k, jnp.concatenate([high, low], axis=0) * scale)


def shards(
    spectrum, depths, currents, slopes, wind_speed, wet_mask, face_owner, face_block,
    freq_weights, angle_weights, transfer_rate,
):
    vmem = pl.BlockSpec(memory_space=pltpu.VMEM)
    dma = pltpu.SemaphoreType.DMA
    return pl.pallas_call(
        kernel,
        out_shape=pltpu.VMEM((FL, DIRS, PTS), F32),
        in_specs=[pl.BlockSpec(memory_space=pl.ANY)] + [vmem] * 10,
        out_specs=vmem,
        scratch_shapes=[
            pltpu.VMEM((FL, DIRS, PTS), F32),
            pltpu.VMEM((NCH, ROWS, LANES), F32),
            pltpu.VMEM((NCH, ROWS, LANES), F32),
            pltpu.VMEM((NCH, 1, LANES), F32),
            pltpu.VMEM((NCH, ROWS, LANES), BF16),
            pltpu.VMEM((NCH, ROWS, LANES), BF16),
            pltpu.VMEM((NFACE, 8, LANES), F32),
            pltpu.VMEM((NCH, LANES + 8, LANES), F32),
            pltpu.VMEM((NCH, LANES + 8, LANES), F32),
            pltpu.VMEM((8, 8, LANES), I32),
            pltpu.VMEM((8, 8, LANES), I32),
            pltpu.VMEM((8, 1, LANES), I32),
            pltpu.VMEM((8, 1, LANES), I32),
            pltpu.VMEM((1, LANES), I32),
            pltpu.SMEM((1, LANES), I32),
            pltpu.VMEM((8, LANES), I32),
            pltpu.SMEM((8, LANES), I32),
            pltpu.VMEM((NB, 8, LANES), I32),
            pltpu.VMEM((NB, 8, LANES), I32),
            pltpu.VMEM((NZ, ROWS // 2, LANES), I32),
            pltpu.VMEM((NZ, ROWS // 2, LANES), I32),
            pltpu.VMEM((NZ, 1, LANES), I32),
            pltpu.VMEM((NZ, 1, LANES), I32),
            pltpu.VMEM((2, 256, 256), BF16),
            pltpu.VMEM((2, 256, 256), BF16),
            pltpu.VMEM((2, 2, GRP, GRP), BF16),
            pltpu.VMEM((2, 2, GRP, GRP), BF16),
            pltpu.VMEM((GRP, 4 * LANES), F32),
            pltpu.VMEM((3, FL, 8, LANES), F32),
            dma, dma((2,)), dma, dma, dma, dma, dma, dma,
            dma((NZ,)), dma((NZ,)), dma((NZ,)), dma((NZ,)), dma((NZ,)), dma((NZ,)),
        ],
        compiler_params=pltpu.CompilerParams(collective_id=0, has_side_effects=True),
    )(
        spectrum, depths.reshape(8, LANES), currents, slopes, wind_speed, wet_mask.reshape(8, LANES),
        face_owner.reshape(1, NFACE), face_block.reshape(1, NFACE), freq_weights, angle_weights,
        transfer_rate.reshape(1, FREQS),
    )


def solution(mesh):
    in_specs = (
        P("spec", None, "blk"), P("blk"), P(None, "blk"), P(None, "blk"), P(None, "blk"), P("blk"),
        P("blk", None), P("blk"), P(), P(), P(),
    )
    return jax.shard_map(
        shards, mesh=mesh, in_specs=in_specs, out_specs=P("spec", None, "blk"), check_vma=False
    )
```

```python
import math

import jax
import jax.numpy as jnp
from jax import lax
from jax.experimental import pallas as pl
from jax.experimental.pallas import tpu as pltpu
from jax.sharding import PartitionSpec as P

MESH = pl.DeviceIdType.MESH
FAR = (4, 3, 5, 2, 6, 1, 7, 0)
F32, BF16, I32 = jnp.float32, jnp.bfloat16, jnp.int32

GRAVITY = 9.81
TIME_STEP = 200.0
CELL_SIZE = 5500.0
LOWEST_FREQ = 0.0418
FREQ_GROWTH = 1.1
WIND_GROWTH = 0.0003
TURN_LIMIT = 0.9

FREQS, FL, DIRS, PTS, LANES = 32, 4, 24, 1024, 128
ROWS = FL * DIRS
NB, NZ, NBLK, NFACE = 64, 8, 16, 64
LAG = 4
NCH = PTS // LANES
GRP = 8 * DIRS
EDGE_SCALE = 26000.0
CODE_MAX = 32767.0
PEAK_SCALE = 1024.0


def iota(shape, axis):
    return lax.broadcasted_iota(I32, shape, axis)


def dot(a, b):
    return jnp.dot(a, b, preferred_element_type=F32)


def dot_nt(a, b):
    return lax.dot_general(a, b, (((1,), (1,)), ((), ())), preferred_element_type=F32)


def by_direction(x):
    return [x.reshape(FREQS, 3, 8, LANES)[:, t].reshape(FREQS * 8, LANES) for t in range(3)]


def to_freq_form(x):
    return jnp.concatenate(by_direction(x), axis=1)


def from_freq_form(x):
    parts = [x[:, t * LANES:(t + 1) * LANES].reshape(FREQS, 1, 8, LANES) for t in range(3)]
    return jnp.concatenate(parts, axis=1).reshape(FREQS * DIRS, LANES)


def to_angle_form(x):
    return jnp.concatenate([x[g * GRP:(g + 1) * GRP] for g in range(4)], axis=1)


def from_angle_form(x):
    return jnp.concatenate([x[:, g * LANES:(g + 1) * LANES] for g in range(4)], axis=0)


def kernel(
    field_hbm, depth_ref, cur_ref, slope_ref, wind_ref, wet_ref, owner_ref, block_ref, fw_ref, aw_ref, rate_ref,
    out_ref,
    field, mv, g1, wetr, lev, lrecv, tab, tab_hi, trw, trs, inw, ins, reqs, line_in, mid, plane_in, asked, ridx, ridx_sm, esend, pool,
    tsend, trecv, ssend, srecv, kf, kt, bd, bt, ratew, shoal,
    in_sem, sm_sem, q_send, q_recv, r_send, r_recv, e_send, e_recv, l_send, l_recv, t_send, t_recv, s_send, s_recv,
):
    me = lax.axis_index("blk")
    z = lax.axis_index("spec")
    barrier = pltpu.get_barrier_semaphore()

    load = pltpu.make_async_copy(field_hbm, field, in_sem)
    load.start()

    x, y, c = me // 16, lax.rem(me // 2, 8), lax.rem(me, 2)
    q = x * 2 + c
    xs = [lax.rem(x + d, 4) * 16 for d in range(4)]
    ys = [lax.rem(y + d, 8) * 2 for d in range(8)]
    cs = [lax.rem(c + d, 2) for d in range(2)]
    plane = [(dx, dc) for dx in (2, 1, 3, 0) for dc in (1, 0) if dx or dc]

    for d in FAR[:-1]:
        for at in ({"blk": xs[0] + ys[d] + cs[0]}, {"spec": lax.rem(z + d, NZ)}):
            pl.semaphore_signal(barrier, inc=1, device_id=at, device_id_type=MESH)
    for dx, dc in plane:
        pl.semaphore_signal(barrier, inc=1, device_id={"blk": xs[dx] + ys[0] + cs[dc]}, device_id_type=MESH)

    own = owner_ref[...]
    ri, ci = iota((NFACE, NFACE), 0), iota((NFACE, NFACE), 1)
    ol = jnp.broadcast_to(own, (NFACE, NFACE))
    os = jnp.sum(jnp.where(ri == ci, ol, 0), axis=1, keepdims=True)
    same = jnp.where(os == ol, 1, 0)
    rank = jnp.sum(jnp.where(ri < ci, same, 0), axis=0, keepdims=True)
    lane = iota((1, NFACE), 1)
    wanted = (block_ref[...] * 4 + jnp.bitwise_xor(jnp.bitwise_and(lane, 3), 1))
    peer = jnp.bitwise_and(ri >> 1, 3) * 16 + (ri >> 3) * 2 + jnp.bitwise_and(ri, 1)
    hit = jnp.where(ol == peer, 1, 0)
    first = jnp.where(rank == 0, wanted, 0)
    second = jnp.where(rank == 1, wanted, 0)
    ask0 = jnp.sum(hit * first, axis=1, keepdims=True)
    ask1 = jnp.sum(hit * second, axis=1, keepdims=True)
    asks = jnp.where(iota((NFACE, LANES), 1) == me, ask0 + 64 * ask1, 0)
    for d in range(8):
        reqs[d] = asks[8 * d:8 * d + 8]
    zpad = jnp.zeros((1, LANES - NFACE), I32)
    si = iota((8, LANES), 0)
    here = own == me
    turn = jnp.where(here, 0, jnp.bitwise_and(rank, 1) * 64)
    turn = jnp.where(lane < 32, turn, 64 - turn)
    wide = [jnp.concatenate([v, zpad], axis=1) for v in (jnp.where(here, NB + wanted, own), turn)]
    faces = jnp.where(si == 0, wide[0], jnp.where(si == 1, wide[1], 0))
    ridx[...] = faces
    move_idx = pltpu.make_async_copy(ridx, ridx_sm, sm_sem.at[0])
    move_idx.start()

    pl.semaphore_wait(barrier, 21)

    for d in FAR[:-1]:
        pltpu.make_async_remote_copy(
            src_ref=reqs.at[lax.rem(y + d, 8)], dst_ref=line_in.at[y], send_sem=q_send, recv_sem=q_recv,
            device_id={"blk": xs[0] + ys[d] + cs[0]}, device_id_type=MESH,
        ).start()
    line_in[y] = reqs[y]

    depth = depth_ref[...]
    base_index = (z * FL).astype(F32)
    freqs = []
    for f in range(FL):
        power = jnp.exp((jnp.full((8, LANES), f, F32) + base_index) * math.log(FREQ_GROWTH))
        rf = power * (2.0 * math.pi * LOWEST_FREQ)
        deep = rf * rf / GRAVITY * depth
        kh = deep / jnp.sqrt(jnp.tanh(deep))
        decay = jnp.exp(-2.0 * kh)
        denom = 1.0 - decay * decay
        phase = rf * depth / kh
        shoal[0, f] = 0.5 * (1.0 + 4.0 * kh * decay / denom) * phase
        shoal[1, f] = 2.0 * rf * decay / denom
        shoal[2, f] = 1.0 / phase
        freqs.append(rf[0:1, :])
    angle = iota((DIRS, LANES), 0).astype(F32) * (2.0 * math.pi / DIRS)
    cosine, sine = jnp.cos(angle), jnp.sin(angle)
    grid_ratio = TIME_STEP / CELL_SIZE
    turn_ratio = TIME_STEP / (2.0 * math.pi / DIRS)
    shape = (FL, DIRS, LANES)
    lane3 = iota(shape, 2)
    col = jnp.bitwise_and(lane3, 7)
    row = jnp.bitwise_and(lax.shift_right_logical(lane3, 3), 7)
    rfcol = jnp.concatenate([f.reshape(1, 1, LANES) for f in freqs], axis=0)
    load.wait()
    lane2 = iota((8, LANES), 1)

    def fold(v, step):
        codes = jnp.minimum(v * EDGE_SCALE + 0.5, 65535.0).astype(I32)
        words = jnp.bitwise_or(codes[:48], jnp.left_shift(codes[48:], 16))
        cell = jnp.bitwise_and(iota((16, LANES), 1), 7) if step == 1 else jnp.bitwise_and(lax.shift_right_logical(iota((16, LANES), 1), 3), 7)
        tail = [pltpu.roll(words[16 * g:16 * g + 16], LANES - step * (6 - 2 * g), axis=1) for g in range(3)]
        tail = jnp.where(cell < 2, tail[0], jnp.where(cell < 4, tail[1], tail[2]))
        return jnp.concatenate([words, tail], axis=0)

    for i in range(4):
        inw[i, :LANES] = jnp.zeros((LANES, LANES), I32)
        ins[i, :LANES] = jnp.zeros((LANES, LANES), I32)
    folded = {}
    for k in (0, 4, 1, 5, 2, 6, 3, 7):
        sl = slice(k * LANES, (k + 1) * LANES)
        e = field[:, :, sl]
        wet = wet_ref[k:k + 1, :].astype(F32)
        group = shoal[0, :, k:k + 1, :]
        turnf = shoal[1, :, k:k + 1, :]
        slow = shoal[2, :, k:k + 1, :]
        cx = (group * cosine[None] + cur_ref[0:1, sl][None]) * grid_ratio * wet[None]
        cy = (group * sine[None] + cur_ref[1:2, sl][None]) * grid_ratio * wet[None]
        bend = sine * slope_ref[0:1, sl] - cosine * slope_ref[1:2, sl]
        ct = jnp.clip(turnf * bend[None] * turn_ratio, -TURN_LIMIT, TURN_LIMIT)
        right = jnp.maximum(cx, 0.0) * e
        left = jnp.maximum(-cx, 0.0) * e
        up = jnp.maximum(cy, 0.0) * e
        down = jnp.maximum(-cy, 0.0) * e
        ahead = jnp.maximum(ct, 0.0) * e
        back = jnp.maximum(-ct, 0.0) * e
        we = jnp.where(col == 0, left, jnp.where(col == 7, right, 0.0)).reshape(ROWS, LANES)
        sn = jnp.where(row == 0, down, jnp.where(row == 7, up, 0.0)).reshape(ROWS, LANES)
        folded[k] = fold(we, 8), fold(sn, 1)
        acc = e - (right + left + up + down + ahead + back)
        acc = acc + jnp.where(col == 0, 0.0, pltpu.roll(right, 1, axis=2))
        acc = acc + jnp.where(col == 7, 0.0, pltpu.roll(left, LANES - 1, axis=2))
        acc = acc + jnp.where(row == 0, 0.0, pltpu.roll(up, 8, axis=2))
        acc = acc + jnp.where(row == 7, 0.0, pltpu.roll(down, LANES - 8, axis=2))
        acc = acc + jnp.concatenate([ahead[:, DIRS - 1:], ahead[:, :DIRS - 1]], axis=1)
        acc = acc + jnp.concatenate([back[:, 1:], back[:, :1]], axis=1)
        mv[k] = acc.reshape(ROWS, LANES)
        along = wind_ref[0:1, sl] * cosine + wind_ref[1:2, sl] * sine
        grow = TIME_STEP * WIND_GROWTH * rfcol * jnp.maximum(along[None] * slow - 1.0, 0.0)
        g1[k] = (wet[None] * (1.0 + grow)).reshape(ROWS, LANES)
        wetr[k] = wet
        if k >= 4:
            trw[k - 4, :LANES] = jnp.transpose(jnp.concatenate([folded[k - 4][0], folded[k][0]], axis=0))
            trs[k - 4, :LANES] = jnp.transpose(jnp.concatenate([folded[k - 4][1], folded[k][1]], axis=0))

    pltpu.make_async_remote_copy(
        src_ref=reqs.at[pl.ds(0, 7)], dst_ref=line_in.at[pl.ds(0, 7)], send_sem=q_send, recv_sem=q_recv,
        device_id={"blk": me}, device_id_type=MESH,
    ).wait()
    gathered = jnp.sum(line_in[...], axis=0)
    for d in range(8):
        mid[d] = gathered[d:d + 1]
    for dx, dc in plane:
        pltpu.make_async_remote_copy(
            src_ref=mid.at[lax.rem(x + dx, 4) * 2 + cs[dc]], dst_ref=plane_in.at[q], send_sem=r_send, recv_sem=r_recv,
            device_id={"blk": xs[dx] + ys[0] + cs[dc]}, device_id_type=MESH,
        ).start()
    plane_in[q] = mid[q]
    for k in range(4):
        for b in range(2):
            base = b * 64
            edges = (
                trw[k, pl.ds(base, 8, stride=8), :], trw[k, pl.ds(base + 7, 8, stride=8), :],
                trs[k, base:base + 8, :], trs[k, base + 56:base + 64, :],
            )
            for side, v in enumerate(edges):
                at = (2 * k + b) * 4 + side
                r = pltpu.roll(v, 64, axis=1)
                for i, (a, o) in ((at, (v, r)), (at + 32, (r, v))):
                    low = jnp.where(lane2 < 64, a, 0)
                    tab[i] = low
                    pool[NB + i] = low
                    tab_hi[i] = jnp.where(lane2 < 64, 0, o)
    pltpu.make_async_remote_copy(
        src_ref=mid.at[pl.ds(0, 7)], dst_ref=plane_in.at[pl.ds(0, 7)], send_sem=r_send, recv_sem=r_recv,
        device_id={"blk": me}, device_id_type=MESH,
    ).wait()
    move_req = pltpu.make_async_copy(plane_in, asked, sm_sem.at[1])
    move_req.start()
    move_req.wait()

    def give(step, p):
        pltpu.make_async_remote_copy(
            src_ref=esend.at[step, pl.ds(0, 6)], dst_ref=pool.at[me, pl.ds(0, 6)], send_sem=e_send, recv_sem=e_recv,
            device_id={"blk": p}, device_id_type=MESH,
        ).start()

    order = [(dx, dy, dc) for dc in (1, 0) for dx in (2, 1, 3, 0) for dy in FAR if dx or dy or dc]
    ready = []
    for step, (dx, dy, dc) in enumerate(order):
        p = xs[dx] + ys[dy] + cs[dc]
        ids = asked[lax.rem(x + dx, 4) * 2 + cs[dc], 0, p]
        low, high = jnp.bitwise_and(ids, 63), jnp.bitwise_and(jnp.right_shift(ids, 6), 63)
        esend[step] = jnp.bitwise_or(tab[low], tab_hi[high])
        ready.append((step, p))
        if len(ready) > LAG:
            give(*ready.pop(0))
    for item in ready:
        give(*item)

    spread = jnp.where(lax.shift_right_logical(iota((256, FREQS), 0), 3) == iota((256, FREQS), 1), 1.0, 0.0).astype(BF16)
    same_i = jnp.bitwise_and(iota((256, 256), 0), 7) == jnp.bitwise_and(iota((256, 256), 1), 7)
    for s in range(2):
        w = fw_ref[s]
        kf[s] = jnp.where(same_i, dot_nt(dot(spread, w).astype(BF16), spread), 0.0).astype(BF16)
        kt[s] = jnp.where(same_i, dot_nt(dot_nt(spread, w).astype(BF16), spread), 0.0).astype(BF16)

    def over(x):
        return lax.shift_right_logical(x * 2731, 16)

    r24 = iota((GRP, DIRS), 0)
    fan = jnp.where(r24 - DIRS * over(r24) == iota((GRP, DIRS), 1), 1.0, 0.0).astype(BF16)
    same_g = over(iota((GRP, GRP), 0)) == over(iota((GRP, GRP), 1))
    for m in range(2):
        for s in range(2):
            a = aw_ref[m, s]
            bd[m, s] = jnp.where(same_g, dot_nt(dot(fan, a).astype(BF16), fan), 0.0).astype(BF16)
            bt[m, s] = jnp.where(same_g, dot_nt(dot_nt(fan, a).astype(BF16), fan), 0.0).astype(BF16)
    for g in range(4):
        pick = over(iota((GRP, FREQS), 0)) + 8 * g == iota((GRP, FREQS), 1)
        column = jnp.sum(jnp.where(pick, rate_ref[...], 0.0), axis=1, keepdims=True)
        ratew[:, g * LANES:(g + 1) * LANES] = jnp.broadcast_to(column, (GRP, LANES))
    pool[me] = jnp.zeros((8, LANES), I32)
    move_idx.wait()

    pltpu.make_async_remote_copy(
        src_ref=esend.at[pl.ds(0, NB - 1), pl.ds(0, 6)], dst_ref=pool.at[pl.ds(0, NB - 1), pl.ds(0, 6)], send_sem=e_send, recv_sem=e_recv,
        device_id={"blk": me}, device_id_type=MESH,
    ).wait()

    def face(j):
        words = pool[ridx_sm[0, j]]
        return jnp.where(ridx_sm[1, j] > 0, pltpu.roll(words, 64, axis=1), words)

    def both(j):
        return jnp.where(lane2 < 64, face(j), face(j + 32))

    lane1 = iota((16, LANES), 1)
    by_row = jnp.bitwise_and(lax.shift_right_logical(lane1, 3), 7) >= 6
    by_col = jnp.bitwise_and(lane1, 7) >= 6

    def unfold(words, step, mask):
        tail = words[48:64]
        parts = [
            jnp.where(mask, pltpu.roll(tail, step * (6 - 2 * g), axis=1), words[16 * g:16 * g + 16]) for g in range(3)
        ]
        return jnp.concatenate(parts, axis=0)

    def finish(slot, m):
        for b in range(2):
            base, j = b * 64, (2 * m + b) * 4
            inw[slot, pl.ds(base, 8, stride=8), :] = both(j)
            inw[slot, pl.ds(base + 7, 8, stride=8), :] = both(j + 1)
            ins[slot, base:base + 8, :] = both(j + 2)
            ins[slot, base + 56:base + 64, :] = both(j + 3)
        wide_w, wide_s = jnp.transpose(inw[slot, :LANES]), jnp.transpose(ins[slot, :LANES])
        for h in range(2):
            k = m + 4 * h
            west = unfold(wide_w[64 * h:64 * h + 64], 8, by_row)
            south = unfold(wide_s[64 * h:64 * h + 64], 1, by_col)
            low = jnp.bitwise_and(west, 65535) + jnp.bitwise_and(south, 65535)
            high = lax.shift_right_logical(west, 16) + lax.shift_right_logical(south, 16)
            codes = jnp.concatenate([low, high], axis=0).astype(F32)
            moved = mv[k] + codes * (1.0 / EDGE_SCALE)
            mv[k] = moved
            lev[k] = moved.astype(BF16)

    def level_copy(k):
        return pltpu.make_async_remote_copy(
            src_ref=lev.at[k], dst_ref=lrecv.at[z], send_sem=l_send.at[k], recv_sem=l_recv.at[z],
            device_id={"spec": k}, device_id_type=MESH,
        )

    waiting = ()
    for slot, (o, nexts) in enumerate(((0, (4,)), (3, (3, 7)), (1, (5, 1)), (2, (2, 6)))):
        finish(slot, lax.rem(z + o, 4))
        if slot == 0:
            lrecv[z] = lev[z]
        for d in waiting:
            level_copy(lax.rem(z + d, NZ)).start()
        waiting = nexts
    for d in waiting:
        level_copy(lax.rem(z + d, NZ)).start()
    for k in range(NCH):
        g1[k] = mv[k] * g1[k]

    for o in range(1, NZ):
        k = lax.rem(z + o, NZ)
        pltpu.make_async_remote_copy(
            src_ref=lev.at[k], dst_ref=lrecv.at[k], send_sem=l_send.at[k], recv_sem=l_recv.at[k],
            device_id={"spec": k}, device_id_type=MESH,
        ).wait()

    levels = lrecv[...].reshape(FREQS * DIRS, LANES).astype(F32)
    level_f = to_freq_form(levels).astype(BF16)
    shifted = [to_angle_form(from_freq_form(dot(kf[s], level_f))).astype(BF16) for s in range(2)]
    level_a = to_angle_form(levels)
    square = level_a * level_a
    total = None
    lows = []
    for m in range(2):
        plus, minus = dot(bd[m, 0], shifted[0]), dot(bd[m, 1], shifted[1])
        delta = ratew[...] * (square * (plus + minus) - 2.0 * level_a * plus * minus)
        lows.append(delta.astype(BF16))
        total = delta if total is None else total + delta
    result = None
    for s in range(2):
        backs = dot(bt[0, s], lows[0]) + dot(bt[1, s], lows[1])
        term = dot(kt[s], to_freq_form(from_angle_form(backs)).astype(BF16))
        result = term if result is None else result + term
    result = from_freq_form(result) - 2.0 * from_angle_form(total)
    mv[...] = result.reshape(NZ, ROWS, LANES)

    def ret_copy(k):
        return pltpu.make_async_remote_copy(
            src_ref=tsend.at[k], dst_ref=trecv.at[z], send_sem=t_send.at[k], recv_sem=t_recv.at[z],
            device_id={"spec": k}, device_id_type=MESH,
        )

    def peak_copy(k):
        return pltpu.make_async_remote_copy(
            src_ref=ssend.at[k], dst_ref=srecv.at[z], send_sem=s_send.at[k], recv_sem=s_recv.at[z],
            device_id={"spec": k}, device_id_type=MESH,
        )

    for o in (4, 3, 5, 2, 6, 1, 7):
        k = lax.rem(z + o, NZ)
        t = mv[k]
        peak = jnp.max(jnp.abs(t), axis=0, keepdims=True)
        unit = (peak * PEAK_SCALE).astype(I32) + 1
        y = t * (CODE_MAX * PEAK_SCALE / unit.astype(F32))
        q = (y + jnp.where(y >= 0.0, 0.5, -0.5)).astype(I32)
        tsend[k] = jnp.bitwise_or(jnp.left_shift(q[:ROWS // 2], 16), jnp.bitwise_and(q[ROWS // 2:], 65535))
        ssend[k] = unit
        ret_copy(k).start()
        peak_copy(k).start()

    def emit(k, t):
        at = pl.ds(pl.multiple_of(k * LANES, LANES), LANES)
        out_ref[:, :, at] = (g1[k] + wetr[k] * t).reshape(FL, DIRS, LANES)

    emit(z, mv[z])
    for o in (1, 7, 2, 6, 3, 5, 4):
        k = lax.rem(z + o, NZ)
        for buf, dst, snd, rcv in ((tsend, trecv, t_send, t_recv), (ssend, srecv, s_send, s_recv)):
            pltpu.make_async_remote_copy(
                src_ref=buf.at[k], dst_ref=dst.at[k], send_sem=snd.at[k], recv_sem=rcv.at[k],
                device_id={"spec": k}, device_id_type=MESH,
            ).wait()
        w = trecv[k]
        scale = srecv[k].astype(F32) * (1.0 / (CODE_MAX * PEAK_SCALE))
        high = jnp.right_shift(w, 16).astype(F32)
        low = jnp.right_shift(jnp.left_shift(w, 16), 16).astype(F32)
        emit(k, jnp.concatenate([high, low], axis=0) * scale)


def shards(
    spectrum, depths, currents, slopes, wind_speed, wet_mask, face_owner, face_block,
    freq_weights, angle_weights, transfer_rate,
):
    vmem = pl.BlockSpec(memory_space=pltpu.VMEM)
    dma = pltpu.SemaphoreType.DMA
    return pl.pallas_call(
        kernel,
        out_shape=pltpu.VMEM((FL, DIRS, PTS), F32),
        in_specs=[pl.BlockSpec(memory_space=pl.ANY)] + [vmem] * 10,
        out_specs=vmem,
        scratch_shapes=[
            pltpu.VMEM((FL, DIRS, PTS), F32),
            pltpu.VMEM((NCH, ROWS, LANES), F32),
            pltpu.VMEM((NCH, ROWS, LANES), F32),
            pltpu.VMEM((NCH, 1, LANES), F32),
            pltpu.VMEM((NCH, ROWS, LANES), BF16),
            pltpu.VMEM((NCH, ROWS, LANES), BF16),
            pltpu.VMEM((NFACE, 8, LANES), I32),
            pltpu.VMEM((NFACE, 8, LANES), I32),
            pltpu.VMEM((4, LANES + 8, LANES), I32),
            pltpu.VMEM((4, LANES + 8, LANES), I32),
            pltpu.VMEM((4, LANES + 8, LANES), I32),
            pltpu.VMEM((4, LANES + 8, LANES), I32),
            pltpu.VMEM((8, 8, LANES), I32),
            pltpu.VMEM((8, 8, LANES), I32),
            pltpu.VMEM((8, 1, LANES), I32),
            pltpu.VMEM((8, 1, LANES), I32),
            pltpu.SMEM((8, 1, LANES), I32),
            pltpu.VMEM((8, LANES), I32),
            pltpu.SMEM((8, LANES), I32),
            pltpu.VMEM((NB, 8, LANES), I32),
            pltpu.VMEM((NB + NFACE, 8, LANES), I32),
            pltpu.VMEM((NZ, ROWS // 2, LANES), I32),
            pltpu.VMEM((NZ, ROWS // 2, LANES), I32),
            pltpu.VMEM((NZ, 1, LANES), I32),
            pltpu.VMEM((NZ, 1, LANES), I32),
            pltpu.VMEM((2, 256, 256), BF16),
            pltpu.VMEM((2, 256, 256), BF16),
            pltpu.VMEM((2, 2, GRP, GRP), BF16),
            pltpu.VMEM((2, 2, GRP, GRP), BF16),
            pltpu.VMEM((GRP, 4 * LANES), F32),
            pltpu.VMEM((3, FL, 8, LANES), F32),
            dma, dma((2,)), dma, dma, dma, dma, dma, dma,
            dma((NZ,)), dma((NZ,)), dma((NZ,)), dma((NZ,)), dma((NZ,)), dma((NZ,)),
        ],
        compiler_params=pltpu.CompilerParams(collective_id=0, has_side_effects=True),
    )(
        spectrum, depths.reshape(8, LANES), currents, slopes, wind_speed, wet_mask.reshape(8, LANES),
        face_owner.reshape(1, NFACE), face_block.reshape(1, NFACE), freq_weights, angle_weights,
        transfer_rate.reshape(1, FREQS),
    )


def solution(mesh):
    in_specs = (
        P("spec", None, "blk"), P("blk"), P(None, "blk"), P(None, "blk"), P(None, "blk"), P("blk"),
        P("blk", None), P("blk"), P(), P(), P(),
    )
    return jax.shard_map(
        shards, mesh=mesh, in_specs=in_specs, out_specs=P("spec", None, "blk"), check_vma=False
    )
```

```python
import math

import jax
import jax.numpy as jnp
from jax import lax
from jax.experimental import pallas as pl
from jax.experimental.pallas import tpu as pltpu
from jax.sharding import PartitionSpec as P

MESH = pl.DeviceIdType.MESH
FAR = (4, 3, 5, 2, 6, 1, 7, 0)
F32, BF16, I32 = jnp.float32, jnp.bfloat16, jnp.int32

GRAVITY = 9.81
TIME_STEP = 200.0
CELL_SIZE = 5500.0
LOWEST_FREQ = 0.0418
FREQ_GROWTH = 1.1
WIND_GROWTH = 0.0003
TURN_LIMIT = 0.9

FREQS, FL, DIRS, PTS, LANES = 32, 4, 24, 1024, 128
ROWS = FL * DIRS
NB, NZ, NBLK, NFACE = 64, 8, 16, 64
LAG = 4
NCH = PTS // LANES
GRP = 8 * DIRS
EDGE_SCALE = 26000.0
CODE_MAX = 32767.0
PEAK_SCALE = 1024.0


def iota(shape, axis):
    return lax.broadcasted_iota(I32, shape, axis)


def dot(a, b):
    return jnp.dot(a, b, preferred_element_type=F32)


def dot_nt(a, b):
    return lax.dot_general(a, b, (((1,), (1,)), ((), ())), preferred_element_type=F32)


def by_direction(x):
    return [x.reshape(FREQS, 3, 8, LANES)[:, t].reshape(FREQS * 8, LANES) for t in range(3)]


def to_freq_form(x):
    return jnp.concatenate(by_direction(x), axis=1)


def from_freq_form(x):
    parts = [x[:, t * LANES:(t + 1) * LANES].reshape(FREQS, 1, 8, LANES) for t in range(3)]
    return jnp.concatenate(parts, axis=1).reshape(FREQS * DIRS, LANES)


def to_angle_form(x):
    return jnp.concatenate([x[g * GRP:(g + 1) * GRP] for g in range(4)], axis=1)


def from_angle_form(x):
    return jnp.concatenate([x[:, g * LANES:(g + 1) * LANES] for g in range(4)], axis=0)


def kernel(
    field_hbm, depth_hbm, cur_hbm, slope_hbm, wind_hbm, wet_hbm, owner_hbm, block_hbm, fw_hbm, aw_hbm, rate_hbm,
    out_ref,
    depth_ref, cur_ref, slope_ref, wind_ref, wet_ref, owner_ref, block_ref, fw_ref, aw_ref, rate_ref, op_sem,
    field, mv, g1, wetr, lev, lrecv, tab, tab_hi, trw, trs, inw, ins, reqs, line_in, mid, plane_in, asked, ridx, ridx_sm, esend, pool,
    tsend, trecv, ssend, srecv, kf, kt, bd, bt, ratew, shoal,
    in_sem, sm_sem, q_send, q_recv, r_send, r_recv, e_send, e_recv, l_send, l_recv, t_send, t_recv, s_send, s_recv,
):
    me = lax.axis_index("blk")
    z = lax.axis_index("spec")
    barrier = pltpu.get_barrier_semaphore()

    x, y, c = me // 16, lax.rem(me // 2, 8), lax.rem(me, 2)
    q = x * 2 + c
    xs = [lax.rem(x + d, 4) * 16 for d in range(4)]
    ys = [lax.rem(y + d, 8) * 2 for d in range(8)]
    cs = [lax.rem(c + d, 2) for d in range(2)]
    plane = [(dx, dc) for dx in (2, 1, 3, 0) for dc in (1, 0) if dx or dc]

    for d in FAR[:-1]:
        for at in ({"blk": xs[0] + ys[d] + cs[0]}, {"spec": lax.rem(z + d, NZ)}):
            pl.semaphore_signal(barrier, inc=1, device_id=at, device_id_type=MESH)
    for dx, dc in plane:
        pl.semaphore_signal(barrier, inc=1, device_id={"blk": xs[dx] + ys[0] + cs[dc]}, device_id_type=MESH)

    small = [
        pltpu.make_async_copy(src, dst, op_sem.at[i]) for i, (src, dst) in enumerate((
            (owner_hbm, owner_ref), (block_hbm, block_ref), (depth_hbm, depth_ref), (cur_hbm, cur_ref),
            (slope_hbm, slope_ref), (wind_hbm, wind_ref), (wet_hbm, wet_ref), (fw_hbm, fw_ref), (aw_hbm, aw_ref),
            (rate_hbm, rate_ref),
        ))
    ]
    for copy in small[:3]:
        copy.start()
    load = pltpu.make_async_copy(field_hbm, field, in_sem)
    load.start()
    for copy in small[3:]:
        copy.start()
    small[0].wait()
    small[1].wait()

    own = owner_ref[...]
    ri, ci = iota((NFACE, NFACE), 0), iota((NFACE, NFACE), 1)
    ol = jnp.broadcast_to(own, (NFACE, NFACE))
    os = jnp.sum(jnp.where(ri == ci, ol, 0), axis=1, keepdims=True)
    same = jnp.where(os == ol, 1, 0)
    rank = jnp.sum(jnp.where(ri < ci, same, 0), axis=0, keepdims=True)
    lane = iota((1, NFACE), 1)
    wanted = (block_ref[...] * 4 + jnp.bitwise_xor(jnp.bitwise_and(lane, 3), 1))
    rank_col = jnp.sum(jnp.where(ci < ri, same, 0), axis=1, keepdims=True)
    wanted_col = jnp.sum(jnp.where(ri == ci, wanted, 0), axis=1, keepdims=True)
    ask = jnp.where(rank_col == 0, wanted_col, jnp.where(rank_col == 1, wanted_col * 64, 0))
    li = iota((NFACE, LANES), 1)
    target = (li >> 5) * 16 + jnp.bitwise_and(li >> 4, 1)
    ask = jnp.where(jnp.bitwise_and(li, 15) == y, ask, 0)
    for d in range(8):
        reqs[d] = jnp.sum(jnp.where(os == target + 2 * d, ask, 0), axis=0, keepdims=True)
    zpad = jnp.zeros((1, LANES - NFACE), I32)
    si = iota((8, LANES), 0)
    here = own == me
    turn = jnp.where(here, 0, jnp.bitwise_and(rank, 1) * 64)
    turn = jnp.where(lane < 32, turn, 64 - turn)
    wide = [jnp.concatenate([v, zpad], axis=1) for v in (jnp.where(here, NB + wanted, own), turn)]
    faces = jnp.where(si == 0, wide[0], jnp.where(si == 1, wide[1], 0))
    ridx[...] = faces
    move_idx = pltpu.make_async_copy(ridx, ridx_sm, sm_sem.at[0])
    move_idx.start()

    pl.semaphore_wait(barrier, 21)

    for d in FAR[:-1]:
        pltpu.make_async_remote_copy(
            src_ref=reqs.at[lax.rem(y + d, 8)], dst_ref=line_in.at[y], send_sem=q_send, recv_sem=q_recv,
            device_id={"blk": xs[0] + ys[d] + cs[0]}, device_id_type=MESH,
        ).start()
    line_in[y] = reqs[y]

    small[2].wait()
    depth = depth_ref[...]
    base_index = (z * FL).astype(F32)
    freqs = []
    for f in range(FL):
        power = jnp.exp((jnp.full((8, LANES), f, F32) + base_index) * math.log(FREQ_GROWTH))
        rf = power * (2.0 * math.pi * LOWEST_FREQ)
        deep = rf * rf / GRAVITY * depth
        kh = deep / jnp.sqrt(jnp.tanh(deep))
        decay = jnp.exp(-2.0 * kh)
        denom = 1.0 - decay * decay
        phase = rf * depth / kh
        shoal[0, f] = 0.5 * (1.0 + 4.0 * kh * decay / denom) * phase
        shoal[1, f] = 2.0 * rf * decay / denom
        shoal[2, f] = 1.0 / phase
        freqs.append(rf[0:1, :])
    angle = iota((DIRS, LANES), 0).astype(F32) * (2.0 * math.pi / DIRS)
    cosine, sine = jnp.cos(angle), jnp.sin(angle)
    grid_ratio = TIME_STEP / CELL_SIZE
    turn_ratio = TIME_STEP / (2.0 * math.pi / DIRS)
    shape = (FL, DIRS, LANES)
    lane3 = iota(shape, 2)
    col = jnp.bitwise_and(lane3, 7)
    row = jnp.bitwise_and(lax.shift_right_logical(lane3, 3), 7)
    rfcol = jnp.concatenate([f.reshape(1, 1, LANES) for f in freqs], axis=0)
    for copy in small[3:7]:
        copy.wait()
    load.wait()
    lane2 = iota((8, LANES), 1)

    def fold(v, step):
        codes = jnp.minimum(v * EDGE_SCALE + 0.5, 65535.0).astype(I32)
        words = jnp.bitwise_or(codes[:48], jnp.left_shift(codes[48:], 16))
        cell = jnp.bitwise_and(iota((16, LANES), 1), 7) if step == 1 else jnp.bitwise_and(lax.shift_right_logical(iota((16, LANES), 1), 3), 7)
        tail = [pltpu.roll(words[16 * g:16 * g + 16], LANES - step * (6 - 2 * g), axis=1) for g in range(3)]
        tail = jnp.where(cell < 2, tail[0], jnp.where(cell < 4, tail[1], tail[2]))
        return jnp.concatenate([words, tail], axis=0)

    for i in range(4):
        inw[i, :LANES] = jnp.zeros((LANES, LANES), I32)
        ins[i, :LANES] = jnp.zeros((LANES, LANES), I32)
    folded = {}
    for k in (0, 4, 1, 5, 2, 6, 3, 7):
        sl = slice(k * LANES, (k + 1) * LANES)
        e = field[:, :, sl]
        wet = wet_ref[k:k + 1, :].astype(F32)
        group = shoal[0, :, k:k + 1, :]
        turnf = shoal[1, :, k:k + 1, :]
        slow = shoal[2, :, k:k + 1, :]
        cx = (group * cosine[None] + cur_ref[0:1, sl][None]) * grid_ratio * wet[None]
        cy = (group * sine[None] + cur_ref[1:2, sl][None]) * grid_ratio * wet[None]
        bend = sine * slope_ref[0:1, sl] - cosine * slope_ref[1:2, sl]
        ct = jnp.clip(turnf * bend[None] * turn_ratio, -TURN_LIMIT, TURN_LIMIT)
        right = jnp.maximum(cx, 0.0) * e
        left = jnp.maximum(-cx, 0.0) * e
        up = jnp.maximum(cy, 0.0) * e
        down = jnp.maximum(-cy, 0.0) * e
        ahead = jnp.maximum(ct, 0.0) * e
        back = jnp.maximum(-ct, 0.0) * e
        we = jnp.where(col == 0, left, jnp.where(col == 7, right, 0.0)).reshape(ROWS, LANES)
        sn = jnp.where(row == 0, down, jnp.where(row == 7, up, 0.0)).reshape(ROWS, LANES)
        folded[k] = fold(we, 8), fold(sn, 1)
        acc = e - (right + left + up + down + ahead + back)
        acc = acc + jnp.where(col == 0, 0.0, pltpu.roll(right, 1, axis=2))
        acc = acc + jnp.where(col == 7, 0.0, pltpu.roll(left, LANES - 1, axis=2))
        acc = acc + jnp.where(row == 0, 0.0, pltpu.roll(up, 8, axis=2))
        acc = acc + jnp.where(row == 7, 0.0, pltpu.roll(down, LANES - 8, axis=2))
        acc = acc + jnp.concatenate([ahead[:, DIRS - 1:], ahead[:, :DIRS - 1]], axis=1)
        acc = acc + jnp.concatenate([back[:, 1:], back[:, :1]], axis=1)
        mv[k] = acc.reshape(ROWS, LANES)
        along = wind_ref[0:1, sl] * cosine + wind_ref[1:2, sl] * sine
        grow = TIME_STEP * WIND_GROWTH * rfcol * jnp.maximum(along[None] * slow - 1.0, 0.0)
        g1[k] = (wet[None] * (1.0 + grow)).reshape(ROWS, LANES)
        wetr[k] = wet
        if k >= 4:
            trw[k - 4, :LANES] = jnp.transpose(jnp.concatenate([folded[k - 4][0], folded[k][0]], axis=0))
            trs[k - 4, :LANES] = jnp.transpose(jnp.concatenate([folded[k - 4][1], folded[k][1]], axis=0))

    pltpu.make_async_remote_copy(
        src_ref=reqs.at[pl.ds(0, 7)], dst_ref=line_in.at[pl.ds(0, 7)], send_sem=q_send, recv_sem=q_recv,
        device_id={"blk": me}, device_id_type=MESH,
    ).wait()
    mid[...] = jnp.sum(line_in[...], axis=0)
    for dx, dc in plane:
        pltpu.make_async_remote_copy(
            src_ref=mid, dst_ref=plane_in.at[q], send_sem=r_send, recv_sem=r_recv,
            device_id={"blk": xs[dx] + ys[0] + cs[dc]}, device_id_type=MESH,
        ).start()
    plane_in[q] = mid[...]
    for k in range(4):
        for b in range(2):
            base = b * 64
            edges = (
                trw[k, pl.ds(base, 8, stride=8), :], trw[k, pl.ds(base + 7, 8, stride=8), :],
                trs[k, base:base + 8, :], trs[k, base + 56:base + 64, :],
            )
            for side, v in enumerate(edges):
                at = (2 * k + b) * 4 + side
                r = pltpu.roll(v, 64, axis=1)
                for i, (a, o) in ((at, (v, r)), (at + 32, (r, v))):
                    low = jnp.where(lane2 < 64, a, 0)
                    tab[i] = low
                    pool[NB + i] = low
                    tab_hi[i] = jnp.where(lane2 < 64, 0, o)
    pltpu.make_async_remote_copy(
        src_ref=plane_in.at[pl.ds(0, 7)], dst_ref=plane_in.at[pl.ds(0, 7)], send_sem=r_send, recv_sem=r_recv,
        device_id={"blk": me}, device_id_type=MESH,
    ).wait()
    move_req = pltpu.make_async_copy(plane_in, asked, sm_sem.at[1])
    move_req.start()
    move_req.wait()

    def give(step, p):
        pltpu.make_async_remote_copy(
            src_ref=esend.at[step, pl.ds(0, 6)], dst_ref=pool.at[me, pl.ds(0, 6)], send_sem=e_send, recv_sem=e_recv,
            device_id={"blk": p}, device_id_type=MESH,
        ).start()

    order = [(dx, dy, dc) for dc in (1, 0) for dx in (2, 1, 3, 0) for dy in FAR if dx or dy or dc]
    ready = []
    for step, (dx, dy, dc) in enumerate(order):
        p = xs[dx] + ys[dy] + cs[dc]
        ids = asked[lax.rem(x + dx, 4) * 2 + cs[dc], 0, q * 16 + lax.rem(y + dy, 8)]
        low, high = jnp.bitwise_and(ids, 63), jnp.bitwise_and(jnp.right_shift(ids, 6), 63)
        esend[step] = jnp.bitwise_or(tab[low], tab_hi[high])
        ready.append((step, p))
        if len(ready) > LAG:
            give(*ready.pop(0))
    for item in ready:
        give(*item)

    for copy in small[7:]:
        copy.wait()
    spread = jnp.where(lax.shift_right_logical(iota((256, FREQS), 0), 3) == iota((256, FREQS), 1), 1.0, 0.0).astype(BF16)
    same_i = jnp.bitwise_and(iota((256, 256), 0), 7) == jnp.bitwise_and(iota((256, 256), 1), 7)
    for s in range(2):
        w = fw_ref[s]
        kf[256 * s:256 * s + 256] = jnp.where(same_i, dot_nt(dot(spread, w).astype(BF16), spread), 0.0).astype(BF16)
        kt[:, 256 * s:256 * s + 256] = jnp.where(same_i, dot_nt(dot_nt(spread, w).astype(BF16), spread), 0.0).astype(BF16)

    def over(x):
        return lax.shift_right_logical(x * 2731, 16)

    r24 = iota((GRP, DIRS), 0)
    fan = jnp.where(r24 - DIRS * over(r24) == iota((GRP, DIRS), 1), 1.0, 0.0).astype(BF16)
    same_g = over(iota((GRP, GRP), 0)) == over(iota((GRP, GRP), 1))
    for m in range(2):
        for s in range(2):
            a = aw_ref[m, s]
            bd[s, GRP * m:GRP * m + GRP] = jnp.where(same_g, dot_nt(dot(fan, a).astype(BF16), fan), 0.0).astype(BF16)
            bt[m, GRP * s:GRP * s + GRP] = jnp.where(same_g, dot_nt(dot_nt(fan, a).astype(BF16), fan), 0.0).astype(BF16)
    for g in range(4):
        pick = over(iota((GRP, FREQS), 0)) + 8 * g == iota((GRP, FREQS), 1)
        column = jnp.sum(jnp.where(pick, rate_ref[...], 0.0), axis=1, keepdims=True)
        ratew[:, g * LANES:(g + 1) * LANES] = jnp.broadcast_to(column, (GRP, LANES))
    pool[me] = jnp.zeros((8, LANES), I32)
    move_idx.wait()

    pltpu.make_async_remote_copy(
        src_ref=esend.at[pl.ds(0, NB - 1), pl.ds(0, 6)], dst_ref=pool.at[pl.ds(0, NB - 1), pl.ds(0, 6)], send_sem=e_send, recv_sem=e_recv,
        device_id={"blk": me}, device_id_type=MESH,
    ).wait()

    def face(j):
        words = pool[ridx_sm[0, j]]
        return jnp.where(ridx_sm[1, j] > 0, pltpu.roll(words, 64, axis=1), words)

    def both(j):
        return jnp.where(lane2 < 64, face(j), face(j + 32))

    lane1 = iota((16, LANES), 1)
    by_row = jnp.bitwise_and(lax.shift_right_logical(lane1, 3), 7) >= 6
    by_col = jnp.bitwise_and(lane1, 7) >= 6

    def unfold(words, step, mask):
        tail = words[48:64]
        parts = [
            jnp.where(mask, pltpu.roll(tail, step * (6 - 2 * g), axis=1), words[16 * g:16 * g + 16]) for g in range(3)
        ]
        return jnp.concatenate(parts, axis=0)

    def finish(slot, m):
        for b in range(2):
            base, j = b * 64, (2 * m + b) * 4
            inw[slot, pl.ds(base, 8, stride=8), :] = both(j)
            inw[slot, pl.ds(base + 7, 8, stride=8), :] = both(j + 1)
            ins[slot, base:base + 8, :] = both(j + 2)
            ins[slot, base + 56:base + 64, :] = both(j + 3)
        wide_w, wide_s = jnp.transpose(inw[slot, :LANES]), jnp.transpose(ins[slot, :LANES])
        for h in range(2):
            k = m + 4 * h
            west = unfold(wide_w[64 * h:64 * h + 64], 8, by_row)
            south = unfold(wide_s[64 * h:64 * h + 64], 1, by_col)
            low = jnp.bitwise_and(west, 65535) + jnp.bitwise_and(south, 65535)
            high = lax.shift_right_logical(west, 16) + lax.shift_right_logical(south, 16)
            codes = jnp.concatenate([low, high], axis=0).astype(F32)
            moved = mv[k] + codes * (1.0 / EDGE_SCALE)
            mv[k] = moved
            lev[k] = moved.astype(BF16)

    def level_copy(k):
        return pltpu.make_async_remote_copy(
            src_ref=lev.at[k], dst_ref=lrecv.at[z], send_sem=l_send.at[k], recv_sem=l_recv.at[z],
            device_id={"spec": k}, device_id_type=MESH,
        )

    waiting = ()
    for slot, (o, nexts) in enumerate(((0, (4,)), (3, (3, 7)), (1, (5, 1)), (2, (2, 6)))):
        finish(slot, lax.rem(z + o, 4))
        if slot == 0:
            lrecv[z] = lev[z]
        for d in waiting:
            level_copy(lax.rem(z + d, NZ)).start()
        waiting = nexts
    for d in waiting:
        level_copy(lax.rem(z + d, NZ)).start()
    for k in range(NCH):
        g1[k] = mv[k] * g1[k]

    for o in range(1, NZ):
        k = lax.rem(z + o, NZ)
        pltpu.make_async_remote_copy(
            src_ref=lev.at[k], dst_ref=lrecv.at[k], send_sem=l_send.at[k], recv_sem=l_recv.at[k],
            device_id={"spec": k}, device_id_type=MESH,
        ).wait()

    levels = lrecv[...].reshape(FREQS * DIRS, LANES).astype(F32)
    level_f = to_freq_form(levels).astype(BF16)
    both_shifted = dot(kf[...], level_f)
    shifted = [to_angle_form(from_freq_form(both_shifted[256 * s:256 * s + 256])).astype(BF16) for s in range(2)]
    level_a = to_angle_form(levels)
    square = level_a * level_a
    pluses, minuses = dot(bd[0], shifted[0]), dot(bd[1], shifted[1])
    total = None
    lows = []
    for m in range(2):
        plus, minus = pluses[GRP * m:GRP * m + GRP], minuses[GRP * m:GRP * m + GRP]
        delta = ratew[...] * (square * (plus + minus) - 2.0 * level_a * plus * minus)
        lows.append(delta.astype(BF16))
        total = delta if total is None else total + delta
    backs = dot(bt[0], lows[0]) + dot(bt[1], lows[1])
    backs = [to_freq_form(from_angle_form(backs[GRP * s:GRP * s + GRP])) for s in range(2)]
    result = dot(kt[...], jnp.concatenate(backs, axis=0).astype(BF16))
    result = from_freq_form(result) - 2.0 * from_angle_form(total)
    mv[...] = result.reshape(NZ, ROWS, LANES)

    def ret_copy(k):
        return pltpu.make_async_remote_copy(
            src_ref=tsend.at[k], dst_ref=trecv.at[z], send_sem=t_send.at[k], recv_sem=t_recv.at[z],
            device_id={"spec": k}, device_id_type=MESH,
        )

    def peak_copy(k):
        return pltpu.make_async_remote_copy(
            src_ref=ssend.at[k], dst_ref=srecv.at[z], send_sem=s_send.at[k], recv_sem=s_recv.at[z],
            device_id={"spec": k}, device_id_type=MESH,
        )

    for o in (4, 3, 5, 2, 6, 1, 7):
        k = lax.rem(z + o, NZ)
        t = mv[k]
        peak = jnp.max(jnp.abs(t), axis=0, keepdims=True)
        unit = (peak * PEAK_SCALE).astype(I32) + 1
        y = t * (CODE_MAX * PEAK_SCALE / unit.astype(F32))
        q = (y + jnp.where(y >= 0.0, 0.5, -0.5)).astype(I32)
        tsend[k] = jnp.bitwise_or(jnp.left_shift(q[:ROWS // 2], 16), jnp.bitwise_and(q[ROWS // 2:], 65535))
        ssend[k] = unit
        ret_copy(k).start()
        peak_copy(k).start()

    def emit(k, t):
        at = pl.ds(pl.multiple_of(k * LANES, LANES), LANES)
        out_ref[:, :, at] = (g1[k] + wetr[k] * t).reshape(FL, DIRS, LANES)

    emit(z, mv[z])
    for o in (1, 7, 2, 6, 3, 5, 4):
        k = lax.rem(z + o, NZ)
        for buf, dst, snd, rcv in ((tsend, trecv, t_send, t_recv), (ssend, srecv, s_send, s_recv)):
            pltpu.make_async_remote_copy(
                src_ref=buf.at[k], dst_ref=dst.at[k], send_sem=snd.at[k], recv_sem=rcv.at[k],
                device_id={"spec": k}, device_id_type=MESH,
            ).wait()
        w = trecv[k]
        scale = srecv[k].astype(F32) * (1.0 / (CODE_MAX * PEAK_SCALE))
        high = jnp.right_shift(w, 16).astype(F32)
        low = jnp.right_shift(jnp.left_shift(w, 16), 16).astype(F32)
        emit(k, jnp.concatenate([high, low], axis=0) * scale)


def shards(
    spectrum, depths, currents, slopes, wind_speed, wet_mask, face_owner, face_block,
    freq_weights, angle_weights, transfer_rate,
):
    vmem = pl.BlockSpec(memory_space=pltpu.VMEM)
    dma = pltpu.SemaphoreType.DMA
    return pl.pallas_call(
        kernel,
        out_shape=pltpu.VMEM((FL, DIRS, PTS), F32),
        in_specs=[pl.BlockSpec(memory_space=pl.ANY)] * 11,
        out_specs=vmem,
        scratch_shapes=[
            pltpu.VMEM((8, LANES), F32), pltpu.VMEM((2, PTS), F32), pltpu.VMEM((2, PTS), F32), pltpu.VMEM((2, PTS), F32),
            pltpu.VMEM((8, LANES), I32), pltpu.VMEM((1, NFACE), I32), pltpu.VMEM((1, NFACE), I32),
            pltpu.VMEM((2, FREQS, FREQS), BF16), pltpu.VMEM((2, 2, DIRS, DIRS), BF16), pltpu.VMEM((1, FREQS), F32), dma((10,)),
            pltpu.VMEM((FL, DIRS, PTS), F32),
            pltpu.VMEM((NCH, ROWS, LANES), F32),
            pltpu.VMEM((NCH, ROWS, LANES), F32),
            pltpu.VMEM((NCH, 1, LANES), F32),
            pltpu.VMEM((NCH, ROWS, LANES), BF16),
            pltpu.VMEM((NCH, ROWS, LANES), BF16),
            pltpu.VMEM((NFACE, 8, LANES), I32),
            pltpu.VMEM((NFACE, 8, LANES), I32),
            pltpu.VMEM((4, LANES + 8, LANES), I32),
            pltpu.VMEM((4, LANES + 8, LANES), I32),
            pltpu.VMEM((4, LANES + 8, LANES), I32),
            pltpu.VMEM((4, LANES + 8, LANES), I32),
            pltpu.VMEM((8, 1, LANES), I32),
            pltpu.VMEM((8, 1, LANES), I32),
            pltpu.VMEM((1, LANES), I32),
            pltpu.VMEM((8, 1, LANES), I32),
            pltpu.SMEM((8, 1, LANES), I32),
            pltpu.VMEM((8, LANES), I32),
            pltpu.SMEM((8, LANES), I32),
            pltpu.VMEM((NB, 8, LANES), I32),
            pltpu.VMEM((NB + NFACE, 8, LANES), I32),
            pltpu.VMEM((NZ, ROWS // 2, LANES), I32),
            pltpu.VMEM((NZ, ROWS // 2, LANES), I32),
            pltpu.VMEM((NZ, 1, LANES), I32),
            pltpu.VMEM((NZ, 1, LANES), I32),
            pltpu.VMEM((512, 256), BF16),
            pltpu.VMEM((256, 512), BF16),
            pltpu.VMEM((2, 2 * GRP, GRP), BF16),
            pltpu.VMEM((2, 2 * GRP, GRP), BF16),
            pltpu.VMEM((GRP, 4 * LANES), F32),
            pltpu.VMEM((3, FL, 8, LANES), F32),
            dma, dma((2,)), dma, dma, dma, dma, dma, dma,
            dma((NZ,)), dma((NZ,)), dma((NZ,)), dma((NZ,)), dma((NZ,)), dma((NZ,)),
        ],
        compiler_params=pltpu.CompilerParams(collective_id=0, has_side_effects=True),
    )(
        spectrum, depths.reshape(8, LANES), currents, slopes, wind_speed, wet_mask.reshape(8, LANES),
        face_owner.reshape(1, NFACE), face_block.reshape(1, NFACE), freq_weights, angle_weights,
        transfer_rate.reshape(1, FREQS),
    )


def solution(mesh):
    in_specs = (
        P("spec", None, "blk"), P("blk"), P(None, "blk"), P(None, "blk"), P(None, "blk"), P("blk"),
        P("blk", None), P("blk"), P(), P(), P(),
    )
    return jax.shard_map(
        shards, mesh=mesh, in_specs=in_specs, out_specs=P("spec", None, "blk"), check_vma=False
    )
```

```python
import math

import jax
import jax.numpy as jnp
from jax import lax
from jax.experimental import pallas as pl
from jax.experimental.pallas import tpu as pltpu
from jax.sharding import PartitionSpec as P

MESH = pl.DeviceIdType.MESH
FAR = (4, 3, 5, 2, 6, 1, 7, 0)
F32, BF16, I32 = jnp.float32, jnp.bfloat16, jnp.int32

GRAVITY = 9.81
TIME_STEP = 200.0
CELL_SIZE = 5500.0
LOWEST_FREQ = 0.0418
FREQ_GROWTH = 1.1
WIND_GROWTH = 0.0003
TURN_LIMIT = 0.9

FREQS, FL, DIRS, PTS, LANES = 32, 4, 24, 1024, 128
ROWS = FL * DIRS
NB, NZ, NBLK, NFACE = 64, 8, 16, 64
LAG = 4
NCH = PTS // LANES
GRP = 8 * DIRS
EDGE_SCALE = 26000.0
CODE_MAX = 32767.0
PEAK_SCALE = 1024.0


def iota(shape, axis):
    return lax.broadcasted_iota(I32, shape, axis)


def dot(a, b):
    return jnp.dot(a, b, preferred_element_type=F32)


def dot_nt(a, b):
    return lax.dot_general(a, b, (((1,), (1,)), ((), ())), preferred_element_type=F32)


def by_direction(x):
    return [x.reshape(FREQS, 3, 8, LANES)[:, t].reshape(FREQS * 8, LANES) for t in range(3)]


def to_freq_form(x):
    return jnp.concatenate(by_direction(x), axis=1)


def from_freq_form(x):
    parts = [x[:, t * LANES:(t + 1) * LANES].reshape(FREQS, 1, 8, LANES) for t in range(3)]
    return jnp.concatenate(parts, axis=1).reshape(FREQS * DIRS, LANES)


def to_angle_form(x):
    return jnp.concatenate([x[g * GRP:(g + 1) * GRP] for g in range(4)], axis=1)


def from_angle_form(x):
    return jnp.concatenate([x[:, g * LANES:(g + 1) * LANES] for g in range(4)], axis=0)


def kernel(
    field_hbm, depth_hbm, cur_hbm, slope_hbm, wind_hbm, wet_hbm, owner_hbm, block_hbm, fw_hbm, aw_hbm, rate_hbm,
    out_ref,
    depth_ref, cur_ref, slope_ref, wind_ref, wet_ref, owner_ref, block_ref, fw_ref, aw_ref, rate_ref, op_sem,
    field, mv, g1, wetr, lev, lrecv, tab, tab_hi, trw, trs, inw, ins, reqs, line_in, mid, plane_in, asked, ridx, ridx_sm, esend, pool,
    tsend, trecv, ssend, srecv, kf, kt, bd, bt, ratew, shoal,
    in_sem, sm_sem, q_send, q_recv, r_send, r_recv, e_send, e_recv, l_send, l_recv, t_send, t_recv, s_send, s_recv,
):
    me = lax.axis_index("blk")
    z = lax.axis_index("spec")
    barrier = pltpu.get_barrier_semaphore()

    x, y, c = me // 16, lax.rem(me // 2, 8), lax.rem(me, 2)
    q = x * 2 + c
    xs = [lax.rem(x + d, 4) * 16 for d in range(4)]
    ys = [lax.rem(y + d, 8) * 2 for d in range(8)]
    cs = [lax.rem(c + d, 2) for d in range(2)]
    plane = [(dx, dc) for dx in (2, 1, 3, 0) for dc in (1, 0) if dx or dc]

    for d in FAR[:-1]:
        for at in ({"blk": xs[0] + ys[d] + cs[0]}, {"spec": lax.rem(z + d, NZ)}):
            pl.semaphore_signal(barrier, inc=1, device_id=at, device_id_type=MESH)
    for dx, dc in plane:
        pl.semaphore_signal(barrier, inc=1, device_id={"blk": xs[dx] + ys[0] + cs[dc]}, device_id_type=MESH)

    small = [
        pltpu.make_async_copy(src, dst, op_sem.at[i]) for i, (src, dst) in enumerate((
            (owner_hbm, owner_ref), (block_hbm, block_ref), (depth_hbm, depth_ref), (cur_hbm, cur_ref),
            (slope_hbm, slope_ref), (wind_hbm, wind_ref), (wet_hbm, wet_ref), (fw_hbm, fw_ref), (aw_hbm, aw_ref),
            (rate_hbm, rate_ref),
        ))
    ]
    for copy in small[:3]:
        copy.start()
    load = pltpu.make_async_copy(field_hbm, field, in_sem)
    load.start()
    for copy in small[3:]:
        copy.start()
    small[0].wait()
    small[1].wait()

    own = owner_ref[...]
    ri, ci = iota((NFACE, NFACE), 0), iota((NFACE, NFACE), 1)
    ol = jnp.broadcast_to(own, (NFACE, NFACE))
    os = jnp.sum(jnp.where(ri == ci, ol, 0), axis=1, keepdims=True)
    same = jnp.where(os == ol, 1, 0)
    rank = jnp.sum(jnp.where(ri < ci, same, 0), axis=0, keepdims=True)
    lane = iota((1, NFACE), 1)
    wanted = (block_ref[...] * 4 + jnp.bitwise_xor(jnp.bitwise_and(lane, 3), 1))
    rank_col = jnp.sum(jnp.where(ci < ri, same, 0), axis=1, keepdims=True)
    wanted_col = jnp.sum(jnp.where(ri == ci, wanted, 0), axis=1, keepdims=True)
    ask = jnp.where(rank_col == 0, wanted_col, jnp.where(rank_col == 1, wanted_col * 64, 0))
    li = iota((NFACE, LANES), 1)
    target = (li >> 5) * 16 + jnp.bitwise_and(li >> 4, 1)
    ask = jnp.where(jnp.bitwise_and(li, 15) == y, ask, 0)
    for d in range(8):
        reqs[d] = jnp.sum(jnp.where(os == target + 2 * d, ask, 0), axis=0, keepdims=True)
    zpad = jnp.zeros((1, LANES - NFACE), I32)
    si = iota((8, LANES), 0)
    here = own == me
    turn = jnp.where(here, 0, jnp.bitwise_and(rank, 1) * 64)
    turn = jnp.where(lane < 32, turn, 64 - turn)
    wide = [jnp.concatenate([v, zpad], axis=1) for v in (jnp.where(here, NB + wanted, own), turn)]
    faces = jnp.where(si == 0, wide[0], jnp.where(si == 1, wide[1], 0))
    ridx[...] = faces
    move_idx = pltpu.make_async_copy(ridx, ridx_sm, sm_sem.at[0])
    move_idx.start()

    pl.semaphore_wait(barrier, 21)

    for d in FAR[:-1]:
        pltpu.make_async_remote_copy(
            src_ref=reqs.at[lax.rem(y + d, 8)], dst_ref=line_in.at[y], send_sem=q_send, recv_sem=q_recv,
            device_id={"blk": xs[0] + ys[d] + cs[0]}, device_id_type=MESH,
        ).start()
    line_in[y] = reqs[y]

    small[2].wait()
    depth = depth_ref[...]
    base_index = (z * FL).astype(F32)
    freqs = []
    for f in range(FL):
        power = jnp.exp((jnp.full((8, LANES), f, F32) + base_index) * math.log(FREQ_GROWTH))
        rf = power * (2.0 * math.pi * LOWEST_FREQ)
        deep = rf * rf / GRAVITY * depth
        kh = deep / jnp.sqrt(jnp.tanh(deep))
        decay = jnp.exp(-2.0 * kh)
        denom = 1.0 - decay * decay
        phase = rf * depth / kh
        shoal[0, f] = 0.5 * (1.0 + 4.0 * kh * decay / denom) * phase
        shoal[1, f] = 2.0 * rf * decay / denom
        shoal[2, f] = 1.0 / phase
        freqs.append(rf[0:1, :])
    angle = iota((DIRS, LANES), 0).astype(F32) * (2.0 * math.pi / DIRS)
    cosine, sine = jnp.cos(angle), jnp.sin(angle)
    grid_ratio = TIME_STEP / CELL_SIZE
    turn_ratio = TIME_STEP / (2.0 * math.pi / DIRS)
    shape = (FL, DIRS, LANES)
    lane3 = iota(shape, 2)
    col = jnp.bitwise_and(lane3, 7)
    row = jnp.bitwise_and(lax.shift_right_logical(lane3, 3), 7)
    rfcol = jnp.concatenate([f.reshape(1, 1, LANES) for f in freqs], axis=0)
    for copy in small[3:7]:
        copy.wait()
    load.wait()
    lane2 = iota((8, LANES), 1)

    def fold(v, step):
        codes = jnp.minimum(v * EDGE_SCALE + 0.5, 65535.0).astype(I32)
        words = jnp.bitwise_or(codes[:48], jnp.left_shift(codes[48:], 16))
        cell = jnp.bitwise_and(iota((16, LANES), 1), 7) if step == 1 else jnp.bitwise_and(lax.shift_right_logical(iota((16, LANES), 1), 3), 7)
        tail = [pltpu.roll(words[16 * g:16 * g + 16], LANES - step * (6 - 2 * g), axis=1) for g in range(3)]
        tail = jnp.where(cell < 2, tail[0], jnp.where(cell < 4, tail[1], tail[2]))
        return jnp.concatenate([words, tail], axis=0)

    for i in range(4):
        inw[i, :LANES] = jnp.zeros((LANES, LANES), I32)
        ins[i, :LANES] = jnp.zeros((LANES, LANES), I32)
    folded = {}
    for k in (0, 4, 1, 5, 2, 6, 3, 7):
        sl = slice(k * LANES, (k + 1) * LANES)
        e = field[:, :, sl]
        wet = wet_ref[k:k + 1, :].astype(F32)
        group = shoal[0, :, k:k + 1, :]
        turnf = shoal[1, :, k:k + 1, :]
        slow = shoal[2, :, k:k + 1, :]
        cx = (group * cosine[None] + cur_ref[0:1, sl][None]) * grid_ratio * wet[None]
        cy = (group * sine[None] + cur_ref[1:2, sl][None]) * grid_ratio * wet[None]
        bend = sine * slope_ref[0:1, sl] - cosine * slope_ref[1:2, sl]
        ct = jnp.clip(turnf * bend[None] * turn_ratio, -TURN_LIMIT, TURN_LIMIT)
        right = jnp.maximum(cx, 0.0) * e
        left = jnp.maximum(-cx, 0.0) * e
        up = jnp.maximum(cy, 0.0) * e
        down = jnp.maximum(-cy, 0.0) * e
        ahead = jnp.maximum(ct, 0.0) * e
        back = jnp.maximum(-ct, 0.0) * e
        we = jnp.where(col == 0, left, jnp.where(col == 7, right, 0.0)).reshape(ROWS, LANES)
        sn = jnp.where(row == 0, down, jnp.where(row == 7, up, 0.0)).reshape(ROWS, LANES)
        folded[k] = fold(we, 8), fold(sn, 1)
        acc = e - (right + left + up + down + ahead + back)
        acc = acc + jnp.where(col == 0, 0.0, pltpu.roll(right, 1, axis=2))
        acc = acc + jnp.where(col == 7, 0.0, pltpu.roll(left, LANES - 1, axis=2))
        acc = acc + jnp.where(row == 0, 0.0, pltpu.roll(up, 8, axis=2))
        acc = acc + jnp.where(row == 7, 0.0, pltpu.roll(down, LANES - 8, axis=2))
        acc = acc + jnp.concatenate([ahead[:, DIRS - 1:], ahead[:, :DIRS - 1]], axis=1)
        acc = acc + jnp.concatenate([back[:, 1:], back[:, :1]], axis=1)
        mv[k] = acc.reshape(ROWS, LANES)
        along = wind_ref[0:1, sl] * cosine + wind_ref[1:2, sl] * sine
        grow = TIME_STEP * WIND_GROWTH * rfcol * jnp.maximum(along[None] * slow - 1.0, 0.0)
        g1[k] = (wet[None] * (1.0 + grow)).reshape(ROWS, LANES)
        wetr[k] = wet
        if k >= 4:
            trw[k - 4, :LANES] = jnp.transpose(jnp.concatenate([folded[k - 4][0], folded[k][0]], axis=0))
            trs[k - 4, :LANES] = jnp.transpose(jnp.concatenate([folded[k - 4][1], folded[k][1]], axis=0))

    pltpu.make_async_remote_copy(
        src_ref=reqs.at[pl.ds(0, 7)], dst_ref=line_in.at[pl.ds(0, 7)], send_sem=q_send, recv_sem=q_recv,
        device_id={"blk": me}, device_id_type=MESH,
    ).wait()
    mid[...] = jnp.sum(line_in[...], axis=0)
    for dx, dc in plane:
        pltpu.make_async_remote_copy(
            src_ref=mid, dst_ref=plane_in.at[q], send_sem=r_send, recv_sem=r_recv,
            device_id={"blk": xs[dx] + ys[0] + cs[dc]}, device_id_type=MESH,
        ).start()
    plane_in[q] = mid[...]
    for k in range(4):
        for b in range(2):
            base = b * 64
            edges = (
                trw[k, pl.ds(base, 8, stride=8), :], trw[k, pl.ds(base + 7, 8, stride=8), :],
                trs[k, base:base + 8, :], trs[k, base + 56:base + 64, :],
            )
            for side, v in enumerate(edges):
                at = (2 * k + b) * 4 + side
                r = pltpu.roll(v, 64, axis=1)
                for i, (a, o) in ((at, (v, r)), (at + 32, (r, v))):
                    low = jnp.where(lane2 < 64, a, 0)
                    tab[i] = low
                    pool[NB + i] = low
                    tab_hi[i] = jnp.where(lane2 < 64, 0, o)
    pltpu.make_async_remote_copy(
        src_ref=plane_in.at[pl.ds(0, 7)], dst_ref=plane_in.at[pl.ds(0, 7)], send_sem=r_send, recv_sem=r_recv,
        device_id={"blk": me}, device_id_type=MESH,
    ).wait()
    move_req = pltpu.make_async_copy(plane_in, asked, sm_sem.at[1])
    move_req.start()
    move_req.wait()

    def give(step, p):
        pltpu.make_async_remote_copy(
            src_ref=esend.at[step, pl.ds(0, 6)], dst_ref=pool.at[me, pl.ds(0, 6)], send_sem=e_send, recv_sem=e_recv,
            device_id={"blk": p}, device_id_type=MESH,
        ).start()

    order = [(dx, dy, dc) for dc in (1, 0) for dx in (2, 1, 3, 0) for dy in (4, 0, 3, 7, 5, 1, 2, 6) if dx or dy or dc]
    ready = []
    for step, (dx, dy, dc) in enumerate(order):
        p = xs[dx] + ys[dy] + cs[dc]
        ids = asked[lax.rem(x + dx, 4) * 2 + cs[dc], 0, q * 16 + lax.rem(y + dy, 8)]
        low, high = jnp.bitwise_and(ids, 63), jnp.bitwise_and(jnp.right_shift(ids, 6), 63)
        esend[step] = jnp.bitwise_or(tab[low], tab_hi[high])
        ready.append((step, p))
        if len(ready) > LAG:
            give(*ready.pop(0))
    for item in ready:
        give(*item)

    for copy in small[7:]:
        copy.wait()
    spread = jnp.where(lax.shift_right_logical(iota((256, FREQS), 0), 3) == iota((256, FREQS), 1), 1.0, 0.0).astype(BF16)
    same_i = jnp.bitwise_and(iota((256, 256), 0), 7) == jnp.bitwise_and(iota((256, 256), 1), 7)
    for s in range(2):
        w = fw_ref[s]
        kf[256 * s:256 * s + 256] = jnp.where(same_i, dot_nt(dot(spread, w).astype(BF16), spread), 0.0).astype(BF16)
        kt[:, 256 * s:256 * s + 256] = jnp.where(same_i, dot_nt(dot_nt(spread, w).astype(BF16), spread), 0.0).astype(BF16)

    def over(x):
        return lax.shift_right_logical(x * 2731, 16)

    r24 = iota((GRP, DIRS), 0)
    fan = jnp.where(r24 - DIRS * over(r24) == iota((GRP, DIRS), 1), 1.0, 0.0).astype(BF16)
    same_g = over(iota((GRP, GRP), 0)) == over(iota((GRP, GRP), 1))
    for m in range(2):
        for s in range(2):
            a = aw_ref[m, s]
            bd[s, GRP * m:GRP * m + GRP] = jnp.where(same_g, dot_nt(dot(fan, a).astype(BF16), fan), 0.0).astype(BF16)
            bt[m, GRP * s:GRP * s + GRP] = jnp.where(same_g, dot_nt(dot_nt(fan, a).astype(BF16), fan), 0.0).astype(BF16)
    for g in range(4):
        pick = over(iota((GRP, FREQS), 0)) + 8 * g == iota((GRP, FREQS), 1)
        column = jnp.sum(jnp.where(pick, rate_ref[...], 0.0), axis=1, keepdims=True)
        ratew[:, g * LANES:(g + 1) * LANES] = jnp.broadcast_to(column, (GRP, LANES))
    pool[me] = jnp.zeros((8, LANES), I32)
    move_idx.wait()

    pltpu.make_async_remote_copy(
        src_ref=esend.at[pl.ds(0, NB - 1), pl.ds(0, 6)], dst_ref=pool.at[pl.ds(0, NB - 1), pl.ds(0, 6)], send_sem=e_send, recv_sem=e_recv,
        device_id={"blk": me}, device_id_type=MESH,
    ).wait()

    def face(j):
        words = pool[ridx_sm[0, j]]
        return jnp.where(ridx_sm[1, j] > 0, pltpu.roll(words, 64, axis=1), words)

    def both(j):
        return jnp.where(lane2 < 64, face(j), face(j + 32))

    lane1 = iota((16, LANES), 1)
    by_row = jnp.bitwise_and(lax.shift_right_logical(lane1, 3), 7) >= 6
    by_col = jnp.bitwise_and(lane1, 7) >= 6

    def unfold(words, step, mask):
        tail = words[48:64]
        parts = [
            jnp.where(mask, pltpu.roll(tail, step * (6 - 2 * g), axis=1), words[16 * g:16 * g + 16]) for g in range(3)
        ]
        return jnp.concatenate(parts, axis=0)

    def finish(slot, m, sends):
        for b in range(2):
            base, j = b * 64, (2 * m + b) * 4
            inw[slot, pl.ds(base, 8, stride=8), :] = both(j)
            inw[slot, pl.ds(base + 7, 8, stride=8), :] = both(j + 1)
            ins[slot, base:base + 8, :] = both(j + 2)
            ins[slot, base + 56:base + 64, :] = both(j + 3)
        for d in sends:
            level_copy(lax.rem(z + d, NZ)).start()
        wide_w, wide_s = jnp.transpose(inw[slot, :LANES]), jnp.transpose(ins[slot, :LANES])
        for h in range(2):
            k = m + 4 * h
            west = unfold(wide_w[64 * h:64 * h + 64], 8, by_row)
            south = unfold(wide_s[64 * h:64 * h + 64], 1, by_col)
            low = jnp.bitwise_and(west, 65535) + jnp.bitwise_and(south, 65535)
            high = lax.shift_right_logical(west, 16) + lax.shift_right_logical(south, 16)
            codes = jnp.concatenate([low, high], axis=0).astype(F32)
            moved = mv[k] + codes * (1.0 / EDGE_SCALE)
            mv[k] = moved
            lev[k] = moved.astype(BF16)

    def level_copy(k):
        return pltpu.make_async_remote_copy(
            src_ref=lev.at[k], dst_ref=lrecv.at[z], send_sem=l_send.at[k], recv_sem=l_recv.at[z],
            device_id={"spec": k}, device_id_type=MESH,
        )

    waiting = ()
    for slot, (o, nexts) in enumerate(((0, (4,)), (3, (3, 7)), (1, (5, 1)), (2, (2, 6)))):
        finish(slot, lax.rem(z + o, 4), waiting)
        if slot == 0:
            lrecv[z] = lev[z]
        waiting = nexts
    for d in waiting:
        level_copy(lax.rem(z + d, NZ)).start()
    for k in range(NCH):
        g1[k] = mv[k] * g1[k]

    for o in range(1, NZ):
        k = lax.rem(z + o, NZ)
        pltpu.make_async_remote_copy(
            src_ref=lev.at[k], dst_ref=lrecv.at[k], send_sem=l_send.at[k], recv_sem=l_recv.at[k],
            device_id={"spec": k}, device_id_type=MESH,
        ).wait()

    levels = lrecv[...].reshape(FREQS * DIRS, LANES).astype(F32)
    level_f = to_freq_form(levels).astype(BF16)
    both_shifted = dot(kf[...], level_f)
    shifted = [to_angle_form(from_freq_form(both_shifted[256 * s:256 * s + 256])).astype(BF16) for s in range(2)]
    level_a = to_angle_form(levels)
    square = level_a * level_a
    pluses, minuses = dot(bd[0], shifted[0]), dot(bd[1], shifted[1])
    total = None
    lows = []
    for m in range(2):
        plus, minus = pluses[GRP * m:GRP * m + GRP], minuses[GRP * m:GRP * m + GRP]
        delta = ratew[...] * (square * (plus + minus) - 2.0 * level_a * plus * minus)
        lows.append(delta.astype(BF16))
        total = delta if total is None else total + delta
    backs = dot(bt[0], lows[0]) + dot(bt[1], lows[1])
    backs = [to_freq_form(from_angle_form(backs[GRP * s:GRP * s + GRP])) for s in range(2)]
    result = dot(kt[...], jnp.concatenate(backs, axis=0).astype(BF16))
    result = from_freq_form(result) - 2.0 * from_angle_form(total)
    mv[...] = result.reshape(NZ, ROWS, LANES)

    def ret_copy(k):
        return pltpu.make_async_remote_copy(
            src_ref=tsend.at[k], dst_ref=trecv.at[z], send_sem=t_send.at[k], recv_sem=t_recv.at[z],
            device_id={"spec": k}, device_id_type=MESH,
        )

    def peak_copy(k):
        return pltpu.make_async_remote_copy(
            src_ref=ssend.at[k], dst_ref=srecv.at[z], send_sem=s_send.at[k], recv_sem=s_recv.at[z],
            device_id={"spec": k}, device_id_type=MESH,
        )

    for o in (4, 3, 5, 2, 6, 1, 7):
        k = lax.rem(z + o, NZ)
        t = mv[k]
        peak = jnp.max(jnp.abs(t), axis=0, keepdims=True)
        unit = (peak * PEAK_SCALE).astype(I32) + 1
        y = t * (CODE_MAX * PEAK_SCALE / unit.astype(F32))
        q = (y + jnp.where(y >= 0.0, 0.5, -0.5)).astype(I32)
        tsend[k] = jnp.bitwise_or(jnp.left_shift(q[:ROWS // 2], 16), jnp.bitwise_and(q[ROWS // 2:], 65535))
        ssend[k] = unit
        peak_copy(k).start()
        ret_copy(k).start()

    def emit(k, t):
        at = pl.ds(pl.multiple_of(k * LANES, LANES), LANES)
        out_ref[:, :, at] = (g1[k] + wetr[k] * t).reshape(FL, DIRS, LANES)

    emit(z, mv[z])
    for o in (1, 7, 2, 6, 3, 5, 4):
        k = lax.rem(z + o, NZ)
        for buf, dst, snd, rcv in ((tsend, trecv, t_send, t_recv), (ssend, srecv, s_send, s_recv)):
            pltpu.make_async_remote_copy(
                src_ref=buf.at[k], dst_ref=dst.at[k], send_sem=snd.at[k], recv_sem=rcv.at[k],
                device_id={"spec": k}, device_id_type=MESH,
            ).wait()
        w = trecv[k]
        scale = srecv[k].astype(F32) * (1.0 / (CODE_MAX * PEAK_SCALE))
        high = jnp.right_shift(w, 16).astype(F32)
        low = jnp.right_shift(jnp.left_shift(w, 16), 16).astype(F32)
        emit(k, jnp.concatenate([high, low], axis=0) * scale)


def shards(
    spectrum, depths, currents, slopes, wind_speed, wet_mask, face_owner, face_block,
    freq_weights, angle_weights, transfer_rate,
):
    vmem = pl.BlockSpec(memory_space=pltpu.VMEM)
    dma = pltpu.SemaphoreType.DMA
    return pl.pallas_call(
        kernel,
        out_shape=pltpu.VMEM((FL, DIRS, PTS), F32),
        in_specs=[pl.BlockSpec(memory_space=pl.ANY)] * 11,
        out_specs=vmem,
        scratch_shapes=[
            pltpu.VMEM((8, LANES), F32), pltpu.VMEM((2, PTS), F32), pltpu.VMEM((2, PTS), F32), pltpu.VMEM((2, PTS), F32),
            pltpu.VMEM((8, LANES), I32), pltpu.VMEM((1, NFACE), I32), pltpu.VMEM((1, NFACE), I32),
            pltpu.VMEM((2, FREQS, FREQS), BF16), pltpu.VMEM((2, 2, DIRS, DIRS), BF16), pltpu.VMEM((1, FREQS), F32), dma((10,)),
            pltpu.VMEM((FL, DIRS, PTS), F32),
            pltpu.VMEM((NCH, ROWS, LANES), F32),
            pltpu.VMEM((NCH, ROWS, LANES), F32),
            pltpu.VMEM((NCH, 1, LANES), F32),
            pltpu.VMEM((NCH, ROWS, LANES), BF16),
            pltpu.VMEM((NCH, ROWS, LANES), BF16),
            pltpu.VMEM((NFACE, 8, LANES), I32),
            pltpu.VMEM((NFACE, 8, LANES), I32),
            pltpu.VMEM((4, LANES + 8, LANES), I32),
            pltpu.VMEM((4, LANES + 8, LANES), I32),
            pltpu.VMEM((4, LANES + 8, LANES), I32),
            pltpu.VMEM((4, LANES + 8, LANES), I32),
            pltpu.VMEM((8, 1, LANES), I32),
            pltpu.VMEM((8, 1, LANES), I32),
            pltpu.VMEM((1, LANES), I32),
            pltpu.VMEM((8, 1, LANES), I32),
            pltpu.SMEM((8, 1, LANES), I32),
            pltpu.VMEM((8, LANES), I32),
            pltpu.SMEM((8, LANES), I32),
            pltpu.VMEM((NB, 8, LANES), I32),
            pltpu.VMEM((NB + NFACE, 8, LANES), I32),
            pltpu.VMEM((NZ, ROWS // 2, LANES), I32),
            pltpu.VMEM((NZ, ROWS // 2, LANES), I32),
            pltpu.VMEM((NZ, 1, LANES), I32),
            pltpu.VMEM((NZ, 1, LANES), I32),
            pltpu.VMEM((512, 256), BF16),
            pltpu.VMEM((256, 512), BF16),
            pltpu.VMEM((2, 2 * GRP, GRP), BF16),
            pltpu.VMEM((2, 2 * GRP, GRP), BF16),
            pltpu.VMEM((GRP, 4 * LANES), F32),
            pltpu.VMEM((3, FL, 8, LANES), F32),
            dma, dma((2,)), dma, dma, dma, dma, dma, dma,
            dma((NZ,)), dma((NZ,)), dma((NZ,)), dma((NZ,)), dma((NZ,)), dma((NZ,)),
        ],
        compiler_params=pltpu.CompilerParams(collective_id=0, has_side_effects=True),
    )(
        spectrum, depths.reshape(8, LANES), currents, slopes, wind_speed, wet_mask.reshape(8, LANES),
        face_owner.reshape(1, NFACE), face_block.reshape(1, NFACE), freq_weights, angle_weights,
        transfer_rate.reshape(1, FREQS),
    )


def solution(mesh):
    in_specs = (
        P("spec", None, "blk"), P("blk"), P(None, "blk"), P(None, "blk"), P(None, "blk"), P("blk"),
        P("blk", None), P("blk"), P(), P(), P(),
    )
    return jax.shard_map(
        shards, mesh=mesh, in_specs=in_specs, out_specs=P("spec", None, "blk"), check_vma=False
    )
```

```python
import math

import jax
import jax.numpy as jnp
from jax import lax
from jax.experimental import pallas as pl
from jax.experimental.pallas import tpu as pltpu
from jax.sharding import PartitionSpec as P

MESH = pl.DeviceIdType.MESH
FAR = (4, 3, 5, 2, 6, 1, 7, 0)
F32, BF16, I32 = jnp.float32, jnp.bfloat16, jnp.int32

GRAVITY = 9.81
TIME_STEP = 200.0
CELL_SIZE = 5500.0
LOWEST_FREQ = 0.0418
FREQ_GROWTH = 1.1
WIND_GROWTH = 0.0003
TURN_LIMIT = 0.9

FREQS, FL, DIRS, PTS, LANES = 32, 4, 24, 1024, 128
ROWS = FL * DIRS
NB, NZ, NBLK, NFACE = 64, 8, 16, 64
LAG = 4
NCH = PTS // LANES
GRP = 8 * DIRS
EDGE_SCALE = 26000.0
CODE_MAX = 32767.0
PEAK_SCALE = 1024.0


def iota(shape, axis):
    return lax.broadcasted_iota(I32, shape, axis)


def dot(a, b):
    return jnp.dot(a, b, preferred_element_type=F32)


def dot_nt(a, b):
    return lax.dot_general(a, b, (((1,), (1,)), ((), ())), preferred_element_type=F32)


def by_direction(x):
    return [x.reshape(FREQS, 3, 8, LANES)[:, t].reshape(FREQS * 8, LANES) for t in range(3)]


def to_freq_form(x):
    return jnp.concatenate(by_direction(x), axis=1)


def from_freq_form(x):
    parts = [x[:, t * LANES:(t + 1) * LANES].reshape(FREQS, 1, 8, LANES) for t in range(3)]
    return jnp.concatenate(parts, axis=1).reshape(FREQS * DIRS, LANES)


def to_angle_form(x):
    return jnp.concatenate([x[g * GRP:(g + 1) * GRP] for g in range(4)], axis=1)


def from_angle_form(x):
    return jnp.concatenate([x[:, g * LANES:(g + 1) * LANES] for g in range(4)], axis=0)


def kernel(
    field_hbm, depth_hbm, cur_hbm, slope_hbm, wind_hbm, wet_hbm, owner_hbm, block_hbm, fw_hbm, aw_hbm, rate_hbm,
    out_ref,
    depth_ref, cur_ref, slope_ref, wind_ref, wet_ref, owner_ref, block_ref, fw_ref, aw_ref, rate_ref, op_sem,
    field, mv, g1, wetr, lev, lrecv, tab, tab_hi, trw, trs, inw, ins, reqs, line_in, mid, plane_in, asked, ridx, ridx_sm, esend, pool,
    tsend, trecv, ssend, srecv, kf, kt, bd, bt, ratew, shoal,
    in_sem, sm_sem, q_send, q_recv, r_send, r_recv, e_send, e_recv, l_send, l_recv, t_send, t_recv, s_send, s_recv,
):
    me = lax.axis_index("blk")
    z = lax.axis_index("spec")
    barrier = pltpu.get_barrier_semaphore()

    x, y, c = me // 16, lax.rem(me // 2, 8), lax.rem(me, 2)
    q = x * 2 + c
    xs = [lax.rem(x + d, 4) * 16 for d in range(4)]
    ys = [lax.rem(y + d, 8) * 2 for d in range(8)]
    cs = [lax.rem(c + d, 2) for d in range(2)]
    plane = [(dx, dc) for dx in (2, 1, 3, 0) for dc in (1, 0) if dx or dc]

    for d in FAR[:-1]:
        pl.semaphore_signal(barrier, inc=1, device_id={"blk": xs[0] + ys[d] + cs[0]}, device_id_type=MESH)
    for dx, dc in plane:
        pl.semaphore_signal(barrier, inc=1, device_id={"blk": xs[dx] + ys[0] + cs[dc]}, device_id_type=MESH)
    for d in FAR[:-1]:
        pl.semaphore_signal(barrier, inc=1, device_id={"spec": lax.rem(z + d, NZ)}, device_id_type=MESH)

    small = [
        pltpu.make_async_copy(src, dst, op_sem.at[i]) for i, (src, dst) in enumerate((
            (owner_hbm, owner_ref), (block_hbm, block_ref), (depth_hbm, depth_ref), (cur_hbm, cur_ref),
            (slope_hbm, slope_ref), (wind_hbm, wind_ref), (wet_hbm, wet_ref), (fw_hbm, fw_ref), (aw_hbm, aw_ref),
            (rate_hbm, rate_ref),
        ))
    ]
    for copy in small[:3]:
        copy.start()
    load = pltpu.make_async_copy(field_hbm, field, in_sem)
    load.start()
    for copy in small[3:]:
        copy.start()
    small[0].wait()
    small[1].wait()

    own = owner_ref[...]
    ri, ci = iota((NFACE, NFACE), 0), iota((NFACE, NFACE), 1)
    ol = jnp.broadcast_to(own, (NFACE, NFACE))
    os = jnp.sum(jnp.where(ri == ci, ol, 0), axis=1, keepdims=True)
    same = jnp.where(os == ol, 1, 0)
    rank = jnp.sum(jnp.where(ri < ci, same, 0), axis=0, keepdims=True)
    lane = iota((1, NFACE), 1)
    wanted = (block_ref[...] * 4 + jnp.bitwise_xor(jnp.bitwise_and(lane, 3), 1))
    rank_col = jnp.sum(jnp.where(ci < ri, same, 0), axis=1, keepdims=True)
    wanted_col = jnp.sum(jnp.where(ri == ci, wanted, 0), axis=1, keepdims=True)
    ask = jnp.where(rank_col == 0, wanted_col, jnp.where(rank_col == 1, wanted_col * 64, 0))
    li = iota((NFACE, LANES), 1)
    target = (li >> 5) * 16 + jnp.bitwise_and(li >> 4, 1)
    ask = jnp.where(jnp.bitwise_and(li, 15) == y, ask, 0)
    for d in range(8):
        reqs[d] = jnp.sum(jnp.where(os == target + 2 * d, ask, 0), axis=0, keepdims=True)
    zpad = jnp.zeros((1, LANES - NFACE), I32)
    si = iota((8, LANES), 0)
    here = own == me
    turn = jnp.where(here, 0, jnp.bitwise_and(rank, 1) * 64)
    turn = jnp.where(lane < 32, turn, 64 - turn)
    wide = [jnp.concatenate([v, zpad], axis=1) for v in (jnp.where(here, NB + wanted, own), turn)]
    faces = jnp.where(si == 0, wide[0], jnp.where(si == 1, wide[1], 0))
    ridx[...] = faces
    move_idx = pltpu.make_async_copy(ridx, ridx_sm, sm_sem.at[0])
    move_idx.start()

    pl.semaphore_wait(barrier, 21)

    for d in FAR[:-1]:
        pltpu.make_async_remote_copy(
            src_ref=reqs.at[lax.rem(y + d, 8)], dst_ref=line_in.at[y], send_sem=q_send, recv_sem=q_recv,
            device_id={"blk": xs[0] + ys[d] + cs[0]}, device_id_type=MESH,
        ).start()
    line_in[y] = reqs[y]

    small[2].wait()
    depth = depth_ref[...]
    base_index = (z * FL).astype(F32)
    freqs = []
    for f in range(FL):
        power = jnp.exp((jnp.full((8, LANES), f, F32) + base_index) * math.log(FREQ_GROWTH))
        rf = power * (2.0 * math.pi * LOWEST_FREQ)
        deep = rf * rf / GRAVITY * depth
        kh = deep / jnp.sqrt(jnp.tanh(deep))
        decay = jnp.exp(-2.0 * kh)
        denom = 1.0 - decay * decay
        phase = rf * depth / kh
        shoal[0, f] = 0.5 * (1.0 + 4.0 * kh * decay / denom) * phase
        shoal[1, f] = 2.0 * rf * decay / denom
        shoal[2, f] = 1.0 / phase
        freqs.append(rf[0:1, :])
    angle = iota((DIRS, LANES), 0).astype(F32) * (2.0 * math.pi / DIRS)
    cosine, sine = jnp.cos(angle), jnp.sin(angle)
    grid_ratio = TIME_STEP / CELL_SIZE
    turn_ratio = TIME_STEP / (2.0 * math.pi / DIRS)
    shape = (FL, DIRS, LANES)
    lane3 = iota(shape, 2)
    col = jnp.bitwise_and(lane3, 7)
    row = jnp.bitwise_and(lax.shift_right_logical(lane3, 3), 7)
    rfcol = jnp.concatenate([f.reshape(1, 1, LANES) for f in freqs], axis=0)
    for copy in small[3:7]:
        copy.wait()
    load.wait()
    lane2 = iota((8, LANES), 1)

    def fold(v, step):
        codes = jnp.minimum(v * EDGE_SCALE + 0.5, 65535.0).astype(I32)
        words = jnp.bitwise_or(codes[:48], jnp.left_shift(codes[48:], 16))
        cell = jnp.bitwise_and(iota((16, LANES), 1), 7) if step == 1 else jnp.bitwise_and(lax.shift_right_logical(iota((16, LANES), 1), 3), 7)
        tail = [pltpu.roll(words[16 * g:16 * g + 16], LANES - step * (6 - 2 * g), axis=1) for g in range(3)]
        tail = jnp.where(cell < 2, tail[0], jnp.where(cell < 4, tail[1], tail[2]))
        return jnp.concatenate([words, tail], axis=0)

    for i in range(4):
        inw[i, :LANES] = jnp.zeros((LANES, LANES), I32)
        ins[i, :LANES] = jnp.zeros((LANES, LANES), I32)
    folded = {}
    for k in (0, 4, 1, 5, 2, 6, 3, 7):
        sl = slice(k * LANES, (k + 1) * LANES)
        e = field[:, :, sl]
        wet = wet_ref[k:k + 1, :].astype(F32)
        group = shoal[0, :, k:k + 1, :]
        turnf = shoal[1, :, k:k + 1, :]
        slow = shoal[2, :, k:k + 1, :]
        cx = (group * cosine[None] + cur_ref[0:1, sl][None]) * grid_ratio * wet[None]
        cy = (group * sine[None] + cur_ref[1:2, sl][None]) * grid_ratio * wet[None]
        bend = sine * slope_ref[0:1, sl] - cosine * slope_ref[1:2, sl]
        ct = jnp.clip(turnf * bend[None] * turn_ratio, -TURN_LIMIT, TURN_LIMIT)
        right = jnp.maximum(cx, 0.0) * e
        left = jnp.maximum(-cx, 0.0) * e
        up = jnp.maximum(cy, 0.0) * e
        down = jnp.maximum(-cy, 0.0) * e
        ahead = jnp.maximum(ct, 0.0) * e
        back = jnp.maximum(-ct, 0.0) * e
        we = jnp.where(col == 0, left, jnp.where(col == 7, right, 0.0)).reshape(ROWS, LANES)
        sn = jnp.where(row == 0, down, jnp.where(row == 7, up, 0.0)).reshape(ROWS, LANES)
        folded[k] = fold(we, 8), fold(sn, 1)
        acc = e - (right + left + up + down + ahead + back)
        acc = acc + jnp.where(col == 0, 0.0, pltpu.roll(right, 1, axis=2))
        acc = acc + jnp.where(col == 7, 0.0, pltpu.roll(left, LANES - 1, axis=2))
        acc = acc + jnp.where(row == 0, 0.0, pltpu.roll(up, 8, axis=2))
        acc = acc + jnp.where(row == 7, 0.0, pltpu.roll(down, LANES - 8, axis=2))
        acc = acc + jnp.concatenate([ahead[:, DIRS - 1:], ahead[:, :DIRS - 1]], axis=1)
        acc = acc + jnp.concatenate([back[:, 1:], back[:, :1]], axis=1)
        mv[k] = acc.reshape(ROWS, LANES)
        along = wind_ref[0:1, sl] * cosine + wind_ref[1:2, sl] * sine
        grow = TIME_STEP * WIND_GROWTH * rfcol * jnp.maximum(along[None] * slow - 1.0, 0.0)
        g1[k] = (wet[None] * (1.0 + grow)).reshape(ROWS, LANES)
        wetr[k] = wet
        if k >= 4:
            trw[k - 4, :LANES] = jnp.transpose(jnp.concatenate([folded[k - 4][0], folded[k][0]], axis=0))
            trs[k - 4, :LANES] = jnp.transpose(jnp.concatenate([folded[k - 4][1], folded[k][1]], axis=0))

    pltpu.make_async_remote_copy(
        src_ref=reqs.at[pl.ds(0, 7)], dst_ref=line_in.at[pl.ds(0, 7)], send_sem=q_send, recv_sem=q_recv,
        device_id={"blk": me}, device_id_type=MESH,
    ).wait()
    mid[...] = jnp.sum(line_in[...], axis=0)
    for dx, dc in plane:
        pltpu.make_async_remote_copy(
            src_ref=mid, dst_ref=plane_in.at[q], send_sem=r_send, recv_sem=r_recv,
            device_id={"blk": xs[dx] + ys[0] + cs[dc]}, device_id_type=MESH,
        ).start()
    plane_in[q] = mid[...]
    for k in range(4):
        for b in range(2):
            base = b * 64
            edges = (
                trw[k, pl.ds(base, 8, stride=8), :], trw[k, pl.ds(base + 7, 8, stride=8), :],
                trs[k, base:base + 8, :], trs[k, base + 56:base + 64, :],
            )
            for side, v in enumerate(edges):
                at = (2 * k + b) * 4 + side
                r = pltpu.roll(v, 64, axis=1)
                for i, (a, o) in ((at, (v, r)), (at + 32, (r, v))):
                    low = jnp.where(lane2 < 64, a, 0)
                    tab[i] = low
                    pool[NB + i] = low
                    tab_hi[i] = jnp.where(lane2 < 64, 0, o)
    pltpu.make_async_remote_copy(
        src_ref=plane_in.at[pl.ds(0, 7)], dst_ref=plane_in.at[pl.ds(0, 7)], send_sem=r_send, recv_sem=r_recv,
        device_id={"blk": me}, device_id_type=MESH,
    ).wait()
    move_req = pltpu.make_async_copy(plane_in, asked, sm_sem.at[1])
    move_req.start()
    move_req.wait()

    def give(step, p):
        pltpu.make_async_remote_copy(
            src_ref=esend.at[step, pl.ds(0, 6)], dst_ref=pool.at[me, pl.ds(0, 6)], send_sem=e_send, recv_sem=e_recv,
            device_id={"blk": p}, device_id_type=MESH,
        ).start()

    order = [(dx, dy, dc) for dc in (1, 0) for dx in (2, 1, 3, 0) for dy in (4, 0, 3, 7, 5, 1, 2, 6) if dx or dy or dc]
    ready = []
    for step, (dx, dy, dc) in enumerate(order):
        p = xs[dx] + ys[dy] + cs[dc]
        ids = asked[lax.rem(x + dx, 4) * 2 + cs[dc], 0, q * 16 + lax.rem(y + dy, 8)]
        low, high = jnp.bitwise_and(ids, 63), jnp.bitwise_and(jnp.right_shift(ids, 6), 63)
        esend[step] = jnp.bitwise_or(tab[low], tab_hi[high])
        ready.append((step, p))
        if len(ready) > LAG:
            give(*ready.pop(0))
    for item in ready:
        give(*item)

    for copy in small[7:]:
        copy.wait()
    spread = jnp.where(lax.shift_right_logical(iota((256, FREQS), 0), 3) == iota((256, FREQS), 1), 1.0, 0.0).astype(BF16)
    same_i = jnp.bitwise_and(iota((256, 256), 0), 7) == jnp.bitwise_and(iota((256, 256), 1), 7)
    for s in range(2):
        w = fw_ref[s]
        kf[256 * s:256 * s + 256] = jnp.where(same_i, dot_nt(dot(spread, w).astype(BF16), spread), 0.0).astype(BF16)
        kt[:, 256 * s:256 * s + 256] = jnp.where(same_i, dot_nt(dot_nt(spread, w).astype(BF16), spread), 0.0).astype(BF16)

    def over(x):
        return lax.shift_right_logical(x * 2731, 16)

    r24 = iota((GRP, DIRS), 0)
    fan = jnp.where(r24 - DIRS * over(r24) == iota((GRP, DIRS), 1), 1.0, 0.0).astype(BF16)
    same_g = over(iota((GRP, GRP), 0)) == over(iota((GRP, GRP), 1))
    for m in range(2):
        for s in range(2):
            a = aw_ref[m, s]
            bd[s, GRP * m:GRP * m + GRP] = jnp.where(same_g, dot_nt(dot(fan, a).astype(BF16), fan), 0.0).astype(BF16)
            bt[m, GRP * s:GRP * s + GRP] = jnp.where(same_g, dot_nt(dot_nt(fan, a).astype(BF16), fan), 0.0).astype(BF16)
    for g in range(4):
        pick = over(iota((GRP, FREQS), 0)) + 8 * g == iota((GRP, FREQS), 1)
        column = jnp.sum(jnp.where(pick, rate_ref[...], 0.0), axis=1, keepdims=True)
        ratew[:, g * LANES:(g + 1) * LANES] = jnp.broadcast_to(column, (GRP, LANES))
    pool[me] = jnp.zeros((8, LANES), I32)
    move_idx.wait()

    pltpu.make_async_remote_copy(
        src_ref=esend.at[pl.ds(0, NB - 1), pl.ds(0, 6)], dst_ref=pool.at[pl.ds(0, NB - 1), pl.ds(0, 6)], send_sem=e_send, recv_sem=e_recv,
        device_id={"blk": me}, device_id_type=MESH,
    ).wait()

    def face(j):
        words = pool[ridx_sm[0, j]]
        return jnp.where(ridx_sm[1, j] > 0, pltpu.roll(words, 64, axis=1), words)

    def both(j):
        return jnp.where(lane2 < 64, face(j), face(j + 32))

    lane1 = iota((16, LANES), 1)
    by_row = jnp.bitwise_and(lax.shift_right_logical(lane1, 3), 7) >= 6
    by_col = jnp.bitwise_and(lane1, 7) >= 6

    def unfold(words, step, mask):
        tail = words[48:64]
        parts = [
            jnp.where(mask, pltpu.roll(tail, step * (6 - 2 * g), axis=1), words[16 * g:16 * g + 16]) for g in range(3)
        ]
        return jnp.concatenate(parts, axis=0)

    def finish(slot, m, sends):
        for b in range(2):
            base, j = b * 64, (2 * m + b) * 4
            inw[slot, pl.ds(base, 8, stride=8), :] = both(j)
            inw[slot, pl.ds(base + 7, 8, stride=8), :] = both(j + 1)
            ins[slot, base:base + 8, :] = both(j + 2)
            ins[slot, base + 56:base + 64, :] = both(j + 3)
        for d in sends:
            level_copy(lax.rem(z + d, NZ)).start()
        wide_w, wide_s = jnp.transpose(inw[slot, :LANES]), jnp.transpose(ins[slot, :LANES])
        for h in range(2):
            k = m + 4 * h
            west = unfold(wide_w[64 * h:64 * h + 64], 8, by_row)
            south = unfold(wide_s[64 * h:64 * h + 64], 1, by_col)
            low = jnp.bitwise_and(west, 65535) + jnp.bitwise_and(south, 65535)
            high = lax.shift_right_logical(west, 16) + lax.shift_right_logical(south, 16)
            codes = jnp.concatenate([low, high], axis=0).astype(F32)
            moved = mv[k] + codes * (1.0 / EDGE_SCALE)
            mv[k] = moved
            lev[k] = moved.astype(BF16)

    def level_copy(k):
        return pltpu.make_async_remote_copy(
            src_ref=lev.at[k], dst_ref=lrecv.at[z], send_sem=l_send.at[k], recv_sem=l_recv.at[z],
            device_id={"spec": k}, device_id_type=MESH,
        )

    waiting = ()
    for slot, (o, nexts) in enumerate(((0, (4,)), (3, (3, 7)), (1, (5, 1)), (2, (2, 6)))):
        finish(slot, lax.rem(z + o, 4), waiting)
        if slot == 0:
            lrecv[z] = lev[z]
        waiting = nexts
    for d in waiting:
        level_copy(lax.rem(z + d, NZ)).start()
    for k in range(NCH):
        g1[k] = mv[k] * g1[k]

    for o in range(1, NZ):
        k = lax.rem(z + o, NZ)
        pltpu.make_async_remote_copy(
            src_ref=lev.at[k], dst_ref=lrecv.at[k], send_sem=l_send.at[k], recv_sem=l_recv.at[k],
            device_id={"spec": k}, device_id_type=MESH,
        ).wait()

    levels = lrecv[...].reshape(FREQS * DIRS, LANES).astype(F32)
    level_f = to_freq_form(levels).astype(BF16)
    both_shifted = dot(kf[...], level_f)
    shifted = [to_angle_form(from_freq_form(both_shifted[256 * s:256 * s + 256])).astype(BF16) for s in range(2)]
    level_a = to_angle_form(levels)
    square = level_a * level_a
    pluses, minuses = dot(bd[0], shifted[0]), dot(bd[1], shifted[1])
    total = None
    lows = []
    for m in range(2):
        plus, minus = pluses[GRP * m:GRP * m + GRP], minuses[GRP * m:GRP * m + GRP]
        delta = ratew[...] * (square * (plus + minus) - 2.0 * level_a * plus * minus)
        lows.append(delta.astype(BF16))
        total = delta if total is None else total + delta
    backs = dot(bt[0], lows[0]) + dot(bt[1], lows[1])
    backs = [to_freq_form(from_angle_form(backs[GRP * s:GRP * s + GRP])) for s in range(2)]
    result = dot(kt[...], jnp.concatenate(backs, axis=0).astype(BF16))
    result = from_freq_form(result) - 2.0 * from_angle_form(total)
    mv[...] = result.reshape(NZ, ROWS, LANES)

    def ret_copy(k):
        return pltpu.make_async_remote_copy(
            src_ref=tsend.at[k], dst_ref=trecv.at[z], send_sem=t_send.at[k], recv_sem=t_recv.at[z],
            device_id={"spec": k}, device_id_type=MESH,
        )

    def peak_copy(k):
        return pltpu.make_async_remote_copy(
            src_ref=ssend.at[k], dst_ref=srecv.at[z], send_sem=s_send.at[k], recv_sem=s_recv.at[z],
            device_id={"spec": k}, device_id_type=MESH,
        )

    for o in (4, 3, 5, 2, 6, 1, 7):
        k = lax.rem(z + o, NZ)
        t = mv[k]
        peak = jnp.max(jnp.abs(t), axis=0, keepdims=True)
        unit = (peak * PEAK_SCALE).astype(I32) + 1
        y = t * (CODE_MAX * PEAK_SCALE / unit.astype(F32))
        q = (y + jnp.where(y >= 0.0, 0.5, -0.5)).astype(I32)
        tsend[k] = jnp.bitwise_or(jnp.left_shift(q[:ROWS // 2], 16), jnp.bitwise_and(q[ROWS // 2:], 65535))
        ssend[k] = unit
        peak_copy(k).start()
        ret_copy(k).start()

    def emit(k, t):
        at = pl.ds(pl.multiple_of(k * LANES, LANES), LANES)
        out_ref[:, :, at] = (g1[k] + wetr[k] * t).reshape(FL, DIRS, LANES)

    emit(z, mv[z])
    for o in (1, 7, 2, 6, 3, 5, 4):
        k = lax.rem(z + o, NZ)
        for buf, dst, snd, rcv in ((tsend, trecv, t_send, t_recv), (ssend, srecv, s_send, s_recv)):
            pltpu.make_async_remote_copy(
                src_ref=buf.at[k], dst_ref=dst.at[k], send_sem=snd.at[k], recv_sem=rcv.at[k],
                device_id={"spec": k}, device_id_type=MESH,
            ).wait()
        w = trecv[k]
        scale = srecv[k].astype(F32) * (1.0 / (CODE_MAX * PEAK_SCALE))
        high = jnp.right_shift(w, 16).astype(F32)
        low = jnp.right_shift(jnp.left_shift(w, 16), 16).astype(F32)
        emit(k, jnp.concatenate([high, low], axis=0) * scale)


def shards(
    spectrum, depths, currents, slopes, wind_speed, wet_mask, face_owner, face_block,
    freq_weights, angle_weights, transfer_rate,
):
    vmem = pl.BlockSpec(memory_space=pltpu.VMEM)
    dma = pltpu.SemaphoreType.DMA
    return pl.pallas_call(
        kernel,
        out_shape=pltpu.VMEM((FL, DIRS, PTS), F32),
        in_specs=[pl.BlockSpec(memory_space=pl.ANY)] * 11,
        out_specs=vmem,
        scratch_shapes=[
            pltpu.VMEM((8, LANES), F32), pltpu.VMEM((2, PTS), F32), pltpu.VMEM((2, PTS), F32), pltpu.VMEM((2, PTS), F32),
            pltpu.VMEM((8, LANES), I32), pltpu.VMEM((1, NFACE), I32), pltpu.VMEM((1, NFACE), I32),
            pltpu.VMEM((2, FREQS, FREQS), BF16), pltpu.VMEM((2, 2, DIRS, DIRS), BF16), pltpu.VMEM((1, FREQS), F32), dma((10,)),
            pltpu.VMEM((FL, DIRS, PTS), F32),
            pltpu.VMEM((NCH, ROWS, LANES), F32),
            pltpu.VMEM((NCH, ROWS, LANES), F32),
            pltpu.VMEM((NCH, 1, LANES), F32),
            pltpu.VMEM((NCH, ROWS, LANES), BF16),
            pltpu.VMEM((NCH, ROWS, LANES), BF16),
            pltpu.VMEM((NFACE, 8, LANES), I32),
            pltpu.VMEM((NFACE, 8, LANES), I32),
            pltpu.VMEM((4, LANES + 8, LANES), I32),
            pltpu.VMEM((4, LANES + 8, LANES), I32),
            pltpu.VMEM((4, LANES + 8, LANES), I32),
            pltpu.VMEM((4, LANES + 8, LANES), I32),
            pltpu.VMEM((8, 1, LANES), I32),
            pltpu.VMEM((8, 1, LANES), I32),
            pltpu.VMEM((1, LANES), I32),
            pltpu.VMEM((8, 1, LANES), I32),
            pltpu.SMEM((8, 1, LANES), I32),
            pltpu.VMEM((8, LANES), I32),
            pltpu.SMEM((8, LANES), I32),
            pltpu.VMEM((NB, 8, LANES), I32),
            pltpu.VMEM((NB + NFACE, 8, LANES), I32),
            pltpu.VMEM((NZ, ROWS // 2, LANES), I32),
            pltpu.VMEM((NZ, ROWS // 2, LANES), I32),
            pltpu.VMEM((NZ, 1, LANES), I32),
            pltpu.VMEM((NZ, 1, LANES), I32),
            pltpu.VMEM((512, 256), BF16),
            pltpu.VMEM((256, 512), BF16),
            pltpu.VMEM((2, 2 * GRP, GRP), BF16),
            pltpu.VMEM((2, 2 * GRP, GRP), BF16),
            pltpu.VMEM((GRP, 4 * LANES), F32),
            pltpu.VMEM((3, FL, 8, LANES), F32),
            dma, dma((2,)), dma, dma, dma, dma, dma, dma,
            dma((NZ,)), dma((NZ,)), dma((NZ,)), dma((NZ,)), dma((NZ,)), dma((NZ,)),
        ],
        compiler_params=pltpu.CompilerParams(collective_id=0, has_side_effects=True),
    )(
        spectrum, depths.reshape(8, LANES), currents, slopes, wind_speed, wet_mask.reshape(8, LANES),
        face_owner.reshape(1, NFACE), face_block.reshape(1, NFACE), freq_weights, angle_weights,
        transfer_rate.reshape(1, FREQS),
    )


def solution(mesh):
    in_specs = (
        P("spec", None, "blk"), P("blk"), P(None, "blk"), P(None, "blk"), P(None, "blk"), P("blk"),
        P("blk", None), P("blk"), P(), P(), P(),
    )
    return jax.shard_map(
        shards, mesh=mesh, in_specs=in_specs, out_specs=P("spec", None, "blk"), check_vma=False
    )
```

```python
import math

import jax
import jax.numpy as jnp
from jax import lax
from jax.experimental import pallas as pl
from jax.experimental.pallas import tpu as pltpu
from jax.sharding import PartitionSpec as P

MESH = pl.DeviceIdType.MESH
FAR = (4, 3, 5, 2, 6, 1, 7, 0)
F32, BF16, I32 = jnp.float32, jnp.bfloat16, jnp.int32

GRAVITY = 9.81
TIME_STEP = 200.0
CELL_SIZE = 5500.0
LOWEST_FREQ = 0.0418
FREQ_GROWTH = 1.1
WIND_GROWTH = 0.0003
TURN_LIMIT = 0.9

FREQS, FL, DIRS, PTS, LANES = 32, 4, 24, 1024, 128
ROWS = FL * DIRS
NB, NZ, NBLK, NFACE = 64, 8, 16, 64
LAG = 4
NCH = PTS // LANES
GRP = 8 * DIRS
EDGE_SCALE = 26000.0
CODE_MAX = 32767.0
PEAK_SCALE = 1024.0


def iota(shape, axis):
    return lax.broadcasted_iota(I32, shape, axis)


def dot(a, b):
    return jnp.dot(a, b, preferred_element_type=F32)


def dot_nt(a, b):
    return lax.dot_general(a, b, (((1,), (1,)), ((), ())), preferred_element_type=F32)


def by_direction(x):
    return [x.reshape(FREQS, 3, 8, LANES)[:, t].reshape(FREQS * 8, LANES) for t in range(3)]


def to_freq_form(x):
    return jnp.concatenate(by_direction(x), axis=1)


def from_freq_form(x):
    parts = [x[:, t * LANES:(t + 1) * LANES].reshape(FREQS, 1, 8, LANES) for t in range(3)]
    return jnp.concatenate(parts, axis=1).reshape(FREQS * DIRS, LANES)


def to_angle_form(x):
    return jnp.concatenate([x[g * GRP:(g + 1) * GRP] for g in range(4)], axis=1)


def from_angle_form(x):
    return jnp.concatenate([x[:, g * LANES:(g + 1) * LANES] for g in range(4)], axis=0)


def kernel(
    field_hbm, depth_hbm, cur_hbm, slope_hbm, wind_hbm, wet_hbm, owner_hbm, block_hbm, fw_hbm, aw_hbm, rate_hbm,
    out_ref,
    depth_ref, cur_ref, slope_ref, wind_ref, wet_ref, owner_ref, block_ref, fw_ref, aw_ref, rate_ref, op_sem,
    field, mv, g1, wetr, lev, lrecv, tab, tab_hi, trw, trs, inw, ins, reqs, line_in, mid, plane_in, asked, ridx, ridx_sm, esend, pool,
    tsend, trecv, ssend, srecv, kf, kt, bd, bt, ratew, shoal,
    in_sem, sm_sem, q_send, q_recv, r_send, r_recv, e_send, e_recv, l_send, l_recv, t_send, t_recv, s_send, s_recv,
):
    me = lax.axis_index("blk")
    z = lax.axis_index("spec")
    barrier = pltpu.get_barrier_semaphore()

    x, y, c = me // 16, lax.rem(me // 2, 8), lax.rem(me, 2)
    q = x * 2 + c
    xs = [lax.rem(x + d, 4) * 16 for d in range(4)]
    ys = [lax.rem(y + d, 8) * 2 for d in range(8)]
    cs = [lax.rem(c + d, 2) for d in range(2)]
    plane = [(dx, dc) for dx in (2, 1, 3, 0) for dc in (1, 0) if dx or dc]

    for d in FAR[:-1]:
        for at in ({"blk": xs[0] + ys[d] + cs[0]}, {"spec": lax.rem(z + d, NZ)}):
            pl.semaphore_signal(barrier, inc=1, device_id=at, device_id_type=MESH)
    for dx, dc in plane:
        pl.semaphore_signal(barrier, inc=1, device_id={"blk": xs[dx] + ys[0] + cs[dc]}, device_id_type=MESH)

    small = [
        pltpu.make_async_copy(src, dst, op_sem.at[i]) for i, (src, dst) in enumerate((
            (owner_hbm, owner_ref), (block_hbm, block_ref), (depth_hbm, depth_ref), (cur_hbm, cur_ref),
            (slope_hbm, slope_ref), (wind_hbm, wind_ref), (wet_hbm, wet_ref), (fw_hbm, fw_ref), (aw_hbm, aw_ref),
            (rate_hbm, rate_ref),
        ))
    ]
    for copy in small[:3]:
        copy.start()
    load = pltpu.make_async_copy(field_hbm, field, in_sem)
    load.start()
    for copy in small[3:]:
        copy.start()
    small[0].wait()
    small[1].wait()

    own = owner_ref[...]
    ri, ci = iota((NFACE, NFACE), 0), iota((NFACE, NFACE), 1)
    ol = jnp.broadcast_to(own, (NFACE, NFACE))
    os = jnp.sum(jnp.where(ri == ci, ol, 0), axis=1, keepdims=True)
    same = jnp.where(os == ol, 1, 0)
    rank = jnp.sum(jnp.where(ri < ci, same, 0), axis=0, keepdims=True)
    lane = iota((1, NFACE), 1)
    wanted = (block_ref[...] * 4 + jnp.bitwise_xor(jnp.bitwise_and(lane, 3), 1))
    rank_col = jnp.sum(jnp.where(ci < ri, same, 0), axis=1, keepdims=True)
    wanted_col = jnp.sum(jnp.where(ri == ci, wanted, 0), axis=1, keepdims=True)
    ask = jnp.where(rank_col == 0, wanted_col, jnp.where(rank_col == 1, wanted_col * 64, 0))
    li = iota((NFACE, LANES), 1)
    target = (li >> 5) * 16 + jnp.bitwise_and(li >> 4, 1)
    ask = jnp.where(jnp.bitwise_and(li, 15) == y, ask, 0)
    for d in range(8):
        reqs[d] = jnp.sum(jnp.where(os == target + 2 * d, ask, 0), axis=0, keepdims=True)
    zpad = jnp.zeros((1, LANES - NFACE), I32)
    si = iota((8, LANES), 0)
    here = own == me
    turn = jnp.where(here, 0, jnp.bitwise_and(rank, 1) * 64)
    turn = jnp.where(lane < 32, turn, 64 - turn)
    wide = [jnp.concatenate([v, zpad], axis=1) for v in (jnp.where(here, NB + wanted, own), turn)]
    faces = jnp.where(si == 0, wide[0], jnp.where(si == 1, wide[1], 0))
    ridx[...] = faces
    move_idx = pltpu.make_async_copy(ridx, ridx_sm, sm_sem.at[0])
    move_idx.start()

    pl.semaphore_wait(barrier, 21)

    for d in FAR[:-1]:
        pltpu.make_async_remote_copy(
            src_ref=reqs.at[lax.rem(y + d, 8)], dst_ref=line_in.at[y], send_sem=q_send, recv_sem=q_recv,
            device_id={"blk": xs[0] + ys[d] + cs[0]}, device_id_type=MESH,
        ).start()
    line_in[y] = reqs[y]

    small[2].wait()
    depth = depth_ref[...]
    base_index = (z * FL).astype(F32)
    freqs = []
    for f in range(FL):
        power = jnp.exp((jnp.full((8, LANES), f, F32) + base_index) * math.log(FREQ_GROWTH))
        rf = power * (2.0 * math.pi * LOWEST_FREQ)
        deep = rf * rf / GRAVITY * depth
        kh = deep / jnp.sqrt(jnp.tanh(deep))
        decay = jnp.exp(-2.0 * kh)
        denom = 1.0 - decay * decay
        phase = rf * depth / kh
        shoal[0, f] = 0.5 * (1.0 + 4.0 * kh * decay / denom) * phase
        shoal[1, f] = 2.0 * rf * decay / denom
        shoal[2, f] = 1.0 / phase
        freqs.append(rf[0:1, :])
    angle = iota((DIRS, LANES), 0).astype(F32) * (2.0 * math.pi / DIRS)
    cosine, sine = jnp.cos(angle), jnp.sin(angle)
    grid_ratio = TIME_STEP / CELL_SIZE
    turn_ratio = TIME_STEP / (2.0 * math.pi / DIRS)
    shape = (FL, DIRS, LANES)
    lane3 = iota(shape, 2)
    col = jnp.bitwise_and(lane3, 7)
    row = jnp.bitwise_and(lax.shift_right_logical(lane3, 3), 7)
    rfcol = jnp.concatenate([f.reshape(1, 1, LANES) for f in freqs], axis=0)
    for copy in small[3:7]:
        copy.wait()
    load.wait()
    lane2 = iota((8, LANES), 1)

    def fold(v, step):
        codes = jnp.minimum(v * EDGE_SCALE + 0.5, 65535.0).astype(I32)
        words = jnp.bitwise_or(codes[:48], jnp.left_shift(codes[48:], 16))
        cell = jnp.bitwise_and(iota((16, LANES), 1), 7) if step == 1 else jnp.bitwise_and(lax.shift_right_logical(iota((16, LANES), 1), 3), 7)
        tail = [pltpu.roll(words[16 * g:16 * g + 16], LANES - step * (6 - 2 * g), axis=1) for g in range(3)]
        tail = jnp.where(cell < 2, tail[0], jnp.where(cell < 4, tail[1], tail[2]))
        return jnp.concatenate([words, tail], axis=0)

    for i in range(4):
        inw[i, :LANES] = jnp.zeros((LANES, LANES), I32)
        ins[i, :LANES] = jnp.zeros((LANES, LANES), I32)
    folded = {}
    for k in (0, 4, 1, 5, 2, 6, 3, 7):
        sl = slice(k * LANES, (k + 1) * LANES)
        e = field[:, :, sl]
        wet = wet_ref[k:k + 1, :].astype(F32)
        group = shoal[0, :, k:k + 1, :]
        turnf = shoal[1, :, k:k + 1, :]
        slow = shoal[2, :, k:k + 1, :]
        cx = (group * cosine[None] + cur_ref[0:1, sl][None]) * grid_ratio * wet[None]
        cy = (group * sine[None] + cur_ref[1:2, sl][None]) * grid_ratio * wet[None]
        bend = sine * slope_ref[0:1, sl] - cosine * slope_ref[1:2, sl]
        ct = jnp.clip(turnf * bend[None] * turn_ratio, -TURN_LIMIT, TURN_LIMIT)
        right = jnp.maximum(cx, 0.0) * e
        left = jnp.maximum(-cx, 0.0) * e
        up = jnp.maximum(cy, 0.0) * e
        down = jnp.maximum(-cy, 0.0) * e
        ahead = jnp.maximum(ct, 0.0) * e
        back = jnp.maximum(-ct, 0.0) * e
        we = jnp.where(col == 0, left, jnp.where(col == 7, right, 0.0)).reshape(ROWS, LANES)
        sn = jnp.where(row == 0, down, jnp.where(row == 7, up, 0.0)).reshape(ROWS, LANES)
        folded[k] = fold(we, 8), fold(sn, 1)
        acc = e - (right + left + up + down + ahead + back)
        acc = acc + jnp.where(col == 0, 0.0, pltpu.roll(right, 1, axis=2))
        acc = acc + jnp.where(col == 7, 0.0, pltpu.roll(left, LANES - 1, axis=2))
        acc = acc + jnp.where(row == 0, 0.0, pltpu.roll(up, 8, axis=2))
        acc = acc + jnp.where(row == 7, 0.0, pltpu.roll(down, LANES - 8, axis=2))
        acc = acc + jnp.concatenate([ahead[:, DIRS - 1:], ahead[:, :DIRS - 1]], axis=1)
        acc = acc + jnp.concatenate([back[:, 1:], back[:, :1]], axis=1)
        mv[k] = acc.reshape(ROWS, LANES)
        along = wind_ref[0:1, sl] * cosine + wind_ref[1:2, sl] * sine
        grow = TIME_STEP * WIND_GROWTH * rfcol * jnp.maximum(along[None] * slow - 1.0, 0.0)
        g1[k] = (wet[None] * (1.0 + grow)).reshape(ROWS, LANES)
        wetr[k] = wet
        if k >= 4:
            trw[k - 4, :LANES] = jnp.transpose(jnp.concatenate([folded[k - 4][0], folded[k][0]], axis=0))
            trs[k - 4, :LANES] = jnp.transpose(jnp.concatenate([folded[k - 4][1], folded[k][1]], axis=0))

    pltpu.make_async_remote_copy(
        src_ref=reqs.at[pl.ds(0, 7)], dst_ref=line_in.at[pl.ds(0, 7)], send_sem=q_send, recv_sem=q_recv,
        device_id={"blk": me}, device_id_type=MESH,
    ).wait()
    mid[...] = jnp.sum(line_in[...], axis=0)
    for dx, dc in plane:
        pltpu.make_async_remote_copy(
            src_ref=mid, dst_ref=plane_in.at[q], send_sem=r_send, recv_sem=r_recv,
            device_id={"blk": xs[dx] + ys[0] + cs[dc]}, device_id_type=MESH,
        ).start()
    plane_in[q] = mid[...]
    for k in range(4):
        for b in range(2):
            base = b * 64
            edges = (
                trw[k, pl.ds(base, 8, stride=8), :], trw[k, pl.ds(base + 7, 8, stride=8), :],
                trs[k, base:base + 8, :], trs[k, base + 56:base + 64, :],
            )
            for side, v in enumerate(edges):
                at = (2 * k + b) * 4 + side
                r = pltpu.roll(v, 64, axis=1)
                for i, (a, o) in ((at, (v, r)), (at + 32, (r, v))):
                    low = jnp.where(lane2 < 64, a, 0)
                    tab[i] = low
                    pool[NB + i] = low
                    tab_hi[i] = jnp.where(lane2 < 64, 0, o)
    pltpu.make_async_remote_copy(
        src_ref=plane_in.at[pl.ds(0, 7)], dst_ref=plane_in.at[pl.ds(0, 7)], send_sem=r_send, recv_sem=r_recv,
        device_id={"blk": me}, device_id_type=MESH,
    ).wait()
    move_req = pltpu.make_async_copy(plane_in, asked, sm_sem.at[1])
    move_req.start()
    move_req.wait()

    def give(step, p):
        pltpu.make_async_remote_copy(
            src_ref=esend.at[step, pl.ds(0, 6)], dst_ref=pool.at[me, pl.ds(0, 6)], send_sem=e_send, recv_sem=e_recv,
            device_id={"blk": p}, device_id_type=MESH,
        ).start()

    order = [(dx, dy, dc) for dc in (1, 0) for dx in (2, 1, 3, 0) for dy in (4, 0, 3, 7, 5, 1, 2, 6) if dx or dy or dc]
    ready = []
    for step, (dx, dy, dc) in enumerate(order):
        p = xs[dx] + ys[dy] + cs[dc]
        ids = asked[lax.rem(x + dx, 4) * 2 + cs[dc], 0, q * 16 + lax.rem(y + dy, 8)]
        low, high = jnp.bitwise_and(ids, 63), jnp.bitwise_and(jnp.right_shift(ids, 6), 63)
        esend[step] = jnp.bitwise_or(tab[low], tab_hi[high])
        ready.append((step, p))
        if len(ready) > LAG:
            give(*ready.pop(0))
    for item in ready:
        give(*item)

    for copy in small[7:]:
        copy.wait()
    spread = jnp.where(lax.shift_right_logical(iota((256, FREQS), 0), 3) == iota((256, FREQS), 1), 1.0, 0.0).astype(BF16)
    same_i = jnp.bitwise_and(iota((256, 256), 0), 7) == jnp.bitwise_and(iota((256, 256), 1), 7)
    for s in range(2):
        w = fw_ref[s]
        kf[256 * s:256 * s + 256] = jnp.where(same_i, dot_nt(dot(spread, w).astype(BF16), spread), 0.0).astype(BF16)
        kt[:, 256 * s:256 * s + 256] = jnp.where(same_i, dot_nt(dot_nt(spread, w).astype(BF16), spread), 0.0).astype(BF16)

    def over(x):
        return lax.shift_right_logical(x * 2731, 16)

    r24 = iota((GRP, DIRS), 0)
    fan = jnp.where(r24 - DIRS * over(r24) == iota((GRP, DIRS), 1), 1.0, 0.0).astype(BF16)
    same_g = over(iota((GRP, GRP), 0)) == over(iota((GRP, GRP), 1))
    for m in range(2):
        for s in range(2):
            a = aw_ref[m, s]
            bd[s, GRP * m:GRP * m + GRP] = jnp.where(same_g, dot_nt(dot(fan, a).astype(BF16), fan), 0.0).astype(BF16)
            bt[m, GRP * s:GRP * s + GRP] = jnp.where(same_g, dot_nt(dot_nt(fan, a).astype(BF16), fan), 0.0).astype(BF16)
    for g in range(4):
        pick = over(iota((GRP, FREQS), 0)) + 8 * g == iota((GRP, FREQS), 1)
        column = jnp.sum(jnp.where(pick, rate_ref[...], 0.0), axis=1, keepdims=True)
        ratew[:, g * LANES:(g + 1) * LANES] = jnp.broadcast_to(column, (GRP, LANES))
    pool[me] = jnp.zeros((8, LANES), I32)
    move_idx.wait()

    pltpu.make_async_remote_copy(
        src_ref=esend.at[pl.ds(0, NB - 1), pl.ds(0, 6)], dst_ref=pool.at[pl.ds(0, NB - 1), pl.ds(0, 6)], send_sem=e_send, recv_sem=e_recv,
        device_id={"blk": me}, device_id_type=MESH,
    ).wait()

    def face(j):
        words = pool[ridx_sm[0, j]]
        return jnp.where(ridx_sm[1, j] > 0, pltpu.roll(words, 64, axis=1), words)

    def both(j):
        return jnp.where(lane2 < 64, face(j), face(j + 32))

    lane1 = iota((16, LANES), 1)
    by_row = jnp.bitwise_and(lax.shift_right_logical(lane1, 3), 7) >= 6
    by_col = jnp.bitwise_and(lane1, 7) >= 6

    def unfold(words, step, mask):
        tail = words[48:64]
        parts = [
            jnp.where(mask, pltpu.roll(tail, step * (6 - 2 * g), axis=1), words[16 * g:16 * g + 16]) for g in range(3)
        ]
        return jnp.concatenate(parts, axis=0)

    def finish(slot, m, sends):
        for b in range(2):
            base, j = b * 64, (2 * m + b) * 4
            inw[slot, pl.ds(base, 8, stride=8), :] = both(j)
            inw[slot, pl.ds(base + 7, 8, stride=8), :] = both(j + 1)
            ins[slot, base:base + 8, :] = both(j + 2)
            ins[slot, base + 56:base + 64, :] = both(j + 3)
        for d in sends:
            level_copy(lax.rem(z + d, NZ)).start()
        wide_w, wide_s = jnp.transpose(inw[slot, :LANES]), jnp.transpose(ins[slot, :LANES])
        for h in range(2):
            k = m + 4 * h
            west = unfold(wide_w[64 * h:64 * h + 64], 8, by_row)
            south = unfold(wide_s[64 * h:64 * h + 64], 1, by_col)
            low = jnp.bitwise_and(west, 65535) + jnp.bitwise_and(south, 65535)
            high = lax.shift_right_logical(west, 16) + lax.shift_right_logical(south, 16)
            codes = jnp.concatenate([low, high], axis=0).astype(F32)
            moved = mv[k] + codes * (1.0 / EDGE_SCALE)
            mv[k] = moved
            lev[k] = moved.astype(BF16)

    def level_copy(k):
        return pltpu.make_async_remote_copy(
            src_ref=lev.at[k], dst_ref=lrecv.at[z], send_sem=l_send.at[k], recv_sem=l_recv.at[z],
            device_id={"spec": k}, device_id_type=MESH,
        )

    waiting = ()
    for slot, (o, nexts) in enumerate(((0, (4,)), (3, (3, 7)), (1, (5, 1)), (2, (2, 6)))):
        finish(slot, lax.rem(z + o, 4), waiting)
        if slot == 0:
            lrecv[z] = lev[z]
        waiting = nexts
    for d in waiting:
        level_copy(lax.rem(z + d, NZ)).start()
    for k in range(NCH):
        g1[k] = mv[k] * g1[k]

    mv[z] = lrecv[z].astype(F32)
    for o in (1, 7, 2, 6, 3, 5, 4):
        k = lax.rem(z + o, NZ)
        pltpu.make_async_remote_copy(
            src_ref=lev.at[k], dst_ref=lrecv.at[k], send_sem=l_send.at[k], recv_sem=l_recv.at[k],
            device_id={"spec": k}, device_id_type=MESH,
        ).wait()
        mv[k] = lrecv[k].astype(F32)

    levels = mv[...].reshape(FREQS * DIRS, LANES)
    level_f = to_freq_form(levels).astype(BF16)
    both_shifted = dot(kf[...], level_f)
    shifted = [to_angle_form(from_freq_form(both_shifted[256 * s:256 * s + 256])).astype(BF16) for s in range(2)]
    level_a = to_angle_form(levels)
    square = level_a * level_a
    pluses, minuses = dot(bd[0], shifted[0]), dot(bd[1], shifted[1])
    total = None
    lows = []
    for m in range(2):
        plus, minus = pluses[GRP * m:GRP * m + GRP], minuses[GRP * m:GRP * m + GRP]
        delta = ratew[...] * (square * (plus + minus) - 2.0 * level_a * plus * minus)
        lows.append(delta.astype(BF16))
        total = delta if total is None else total + delta
    backs = dot(bt[0], lows[0]) + dot(bt[1], lows[1])
    backs = [to_freq_form(from_angle_form(backs[GRP * s:GRP * s + GRP])) for s in range(2)]
    result = dot(kt[...], jnp.concatenate(backs, axis=0).astype(BF16))
    result = from_freq_form(result) - 2.0 * from_angle_form(total)
    mv[...] = result.reshape(NZ, ROWS, LANES)

    def ret_copy(k):
        return pltpu.make_async_remote_copy(
            src_ref=tsend.at[k], dst_ref=trecv.at[z], send_sem=t_send.at[k], recv_sem=t_recv.at[z],
            device_id={"spec": k}, device_id_type=MESH,
        )

    def peak_copy(k):
        return pltpu.make_async_remote_copy(
            src_ref=ssend.at[k], dst_ref=srecv.at[z], send_sem=s_send.at[k], recv_sem=s_recv.at[z],
            device_id={"spec": k}, device_id_type=MESH,
        )

    for o in (4, 3, 5, 2, 6, 1, 7):
        k = lax.rem(z + o, NZ)
        t = mv[k]
        peak = jnp.max(jnp.abs(t), axis=0, keepdims=True)
        unit = (peak * PEAK_SCALE).astype(I32) + 1
        y = t * (CODE_MAX * PEAK_SCALE / unit.astype(F32))
        q = (y + jnp.where(y >= 0.0, 0.5, -0.5)).astype(I32)
        tsend[k] = jnp.bitwise_or(jnp.left_shift(q[:ROWS // 2], 16), jnp.bitwise_and(q[ROWS // 2:], 65535))
        ssend[k] = unit
        peak_copy(k).start()
        ret_copy(k).start()

    def emit(k, t):
        at = pl.ds(pl.multiple_of(k * LANES, LANES), LANES)
        out_ref[:, :, at] = (g1[k] + wetr[k] * t).reshape(FL, DIRS, LANES)

    emit(z, mv[z])
    for o in (1, 7, 2, 6, 3, 5, 4):
        k = lax.rem(z + o, NZ)
        for buf, dst, snd, rcv in ((tsend, trecv, t_send, t_recv), (ssend, srecv, s_send, s_recv)):
            pltpu.make_async_remote_copy(
                src_ref=buf.at[k], dst_ref=dst.at[k], send_sem=snd.at[k], recv_sem=rcv.at[k],
                device_id={"spec": k}, device_id_type=MESH,
            ).wait()
        w = trecv[k]
        scale = srecv[k].astype(F32) * (1.0 / (CODE_MAX * PEAK_SCALE))
        high = jnp.right_shift(w, 16).astype(F32)
        low = jnp.right_shift(jnp.left_shift(w, 16), 16).astype(F32)
        emit(k, jnp.concatenate([high, low], axis=0) * scale)


def shards(
    spectrum, depths, currents, slopes, wind_speed, wet_mask, face_owner, face_block,
    freq_weights, angle_weights, transfer_rate,
):
    vmem = pl.BlockSpec(memory_space=pltpu.VMEM)
    dma = pltpu.SemaphoreType.DMA
    return pl.pallas_call(
        kernel,
        out_shape=pltpu.VMEM((FL, DIRS, PTS), F32),
        in_specs=[pl.BlockSpec(memory_space=pl.ANY)] * 11,
        out_specs=vmem,
        scratch_shapes=[
            pltpu.VMEM((8, LANES), F32), pltpu.VMEM((2, PTS), F32), pltpu.VMEM((2, PTS), F32), pltpu.VMEM((2, PTS), F32),
            pltpu.VMEM((8, LANES), I32), pltpu.VMEM((1, NFACE), I32), pltpu.VMEM((1, NFACE), I32),
            pltpu.VMEM((2, FREQS, FREQS), BF16), pltpu.VMEM((2, 2, DIRS, DIRS), BF16), pltpu.VMEM((1, FREQS), F32), dma((10,)),
            pltpu.VMEM((FL, DIRS, PTS), F32),
            pltpu.VMEM((NCH, ROWS, LANES), F32),
            pltpu.VMEM((NCH, ROWS, LANES), F32),
            pltpu.VMEM((NCH, 1, LANES), F32),
            pltpu.VMEM((NCH, ROWS, LANES), BF16),
            pltpu.VMEM((NCH, ROWS, LANES), BF16),
            pltpu.VMEM((NFACE, 8, LANES), I32),
            pltpu.VMEM((NFACE, 8, LANES), I32),
            pltpu.VMEM((4, LANES + 8, LANES), I32),
            pltpu.VMEM((4, LANES + 8, LANES), I32),
            pltpu.VMEM((4, LANES + 8, LANES), I32),
            pltpu.VMEM((4, LANES + 8, LANES), I32),
            pltpu.VMEM((8, 1, LANES), I32),
            pltpu.VMEM((8, 1, LANES), I32),
            pltpu.VMEM((1, LANES), I32),
            pltpu.VMEM((8, 1, LANES), I32),
            pltpu.SMEM((8, 1, LANES), I32),
            pltpu.VMEM((8, LANES), I32),
            pltpu.SMEM((8, LANES), I32),
            pltpu.VMEM((NB, 8, LANES), I32),
            pltpu.VMEM((NB + NFACE, 8, LANES), I32),
            pltpu.VMEM((NZ, ROWS // 2, LANES), I32),
            pltpu.VMEM((NZ, ROWS // 2, LANES), I32),
            pltpu.VMEM((NZ, 1, LANES), I32),
            pltpu.VMEM((NZ, 1, LANES), I32),
            pltpu.VMEM((512, 256), BF16),
            pltpu.VMEM((256, 512), BF16),
            pltpu.VMEM((2, 2 * GRP, GRP), BF16),
            pltpu.VMEM((2, 2 * GRP, GRP), BF16),
            pltpu.VMEM((GRP, 4 * LANES), F32),
            pltpu.VMEM((3, FL, 8, LANES), F32),
            dma, dma((2,)), dma, dma, dma, dma, dma, dma,
            dma((NZ,)), dma((NZ,)), dma((NZ,)), dma((NZ,)), dma((NZ,)), dma((NZ,)),
        ],
        compiler_params=pltpu.CompilerParams(collective_id=0, has_side_effects=True),
    )(
        spectrum, depths.reshape(8, LANES), currents, slopes, wind_speed, wet_mask.reshape(8, LANES),
        face_owner.reshape(1, NFACE), face_block.reshape(1, NFACE), freq_weights, angle_weights,
        transfer_rate.reshape(1, FREQS),
    )


def solution(mesh):
    in_specs = (
        P("spec", None, "blk"), P("blk"), P(None, "blk"), P(None, "blk"), P(None, "blk"), P("blk"),
        P("blk", None), P("blk"), P(), P(), P(),
    )
    return jax.shard_map(
        shards, mesh=mesh, in_specs=in_specs, out_specs=P("spec", None, "blk"), check_vma=False
    )
```
